128 devices in a mesh: row: 8 (over z_hi, x), col: 16 (over z_lo, y, core).
Axes of the slice: x: 4, y: 4, z: 4 (z_hi: 2, z_lo: 2; z = z_hi * 2 + z_lo), core: 2. Of those that a mesh axis runs over, the one named last changes fastest.
Arguments:
- docs: bfloat16 [16384, 4, 896], P(('row', 'col')), may hold values from -6 to 6
- routes: int32 [16384, 1], P(('row', 'col')), may hold values from 0 to 127; in each aligned block of 128 rows (0 to 127, 128 to 255, ...) at most 2 rows name the same one
- level_one: float32 [8, 896, 896], P('row', 'col'), may hold values from -6 to 6
- level_two: float32 [16, 896, 896], P('col', 'row'), may hold values from -6 to 6
- moment_one: float32 [8, 896, 896], P('row', 'col'), may hold values from -18 to 18
- moment_two: float32 [16, 896, 896], P('col', 'row'), may hold values from -18 to 18
Outputs:
- new_one: float32 [8, 896, 896], P('row', 'col')
- new_two: float32 [16, 896, 896], P('col', 'row')
- next_moment_one: float32 [8, 896, 896], P('row', 'col')
- next_moment_two: float32 [16, 896, 896], P('col', 'row')
The draws below stay inside these ranges and needn't reach their ends.
Inputs may be any that keep to these rules, and one draw needn't show every extreme that they name: `routes`: each block names one path; among the 128 blocks of one device no path is named more than 2 times, and every path is named by some block.
All inputs are finite; a program needn't handle non-finite values.
Results may differ from the reference program's by a relative error of at most 0.017.
Values may be sent and summed in bfloat16 or wider, within the bound.
No kernel may reach another device: no remote copies, remote signals or barrier semaphores. Data moves between devices by JAX's collectives and lax.ppermute only.
A program may use at most 128 MiB of HBM per device.

```python
import math
import jax
import jax.numpy as jnp
import numpy as np
from jax import lax

D = 896
BLOCK = 4
STEPS = 3
DOCS = 128
PATHS = 128
CAP = 2
TOTAL_DOCS = 16384
N_ROW = 8
N_COL = 16


def block_scale(stream_key, dims, shards, smallest, high):
    level, own = 1.0, jax.random.fold_in(stream_key, 6)
    for axis_at, parts in shards:
        heights = jnp.exp(jax.random.uniform(jax.random.fold_in(own, axis_at), (parts,), jnp.float32, smallest / len(shards), high / len(shards)))
        level = level * jnp.repeat(heights, dims[axis_at] // parts).reshape([-1 if axis == axis_at else 1 for axis in range(len(dims))])
    return level


def assign_block(rng, own, number, rows, number_of, top, limit, slope):
    ranking = jax.random.permutation(rng, number_of)
    heavy_load, common = portions_of(number_of, rows * top, limit, slope, True), portions_of(number_of, rows * top, limit, slope, False)
    places = jnp.arange(number_of)

    def named(tallies, rotation):
        used = int((tallies > 0).sum())
        fixed = max(1, used // 4)
        shifted = fixed + (places - fixed + rotation * (used - fixed)) % max(1, number_of - fixed)
        return jnp.zeros((number_of,), jnp.int32).at[ranking[jnp.where(places < fixed, places, shifted)]].set(jnp.asarray(tallies, jnp.int32))

    tallies = jnp.where(number % 4 == 0, named(heavy_load, number // 4), named(common, number - number // 4 - 1))
    mixed = jax.random.permutation(jax.random.fold_in(own, 3), number_of)
    donor, taker = mixed[0:number_of // 2 * 2:2], mixed[1:number_of // 2 * 2:2]
    margin = jnp.minimum(tallies[donor] - 1, limit - tallies[taker]) // 2
    margin = jnp.where((donor == ranking[0]) | (taker == ranking[0]) | (tallies[taker] == 0), 0, jnp.maximum(margin, 0))
    shifted = jax.random.randint(jax.random.fold_in(own, 4), (number_of // 2,), 0, 1 << 20) % (margin + 1)
    tallies = tallies.at[donor].add(-shifted).at[taker].add(shifted)
    items = jnp.searchsorted(jnp.cumsum(tallies), jnp.arange(rows * top), side="right").astype(jnp.int32)
    table = items.reshape(top, rows).T
    table = table[jax.random.permutation(jax.random.fold_in(own, 1), rows)]
    rotation = jax.random.randint(jax.random.fold_in(own, 2), (rows, 1), 0, top)
    return jnp.take_along_axis(table, (jnp.arange(top)[None, :] + rotation) % top, axis=1)


def portions_of(count, total, limit, lean, full):
    portions = [(1 << 20) // math.isqrt(grade ** lean) + 1 for grade in range(1, count + 1)]
    largest = limit if full else min(limit, max(-(-total // count), total * portions[0] // sum(portions)))
    least = 1 if total - largest >= count - 1 else 0
    counts, spare = [largest] + [least] * (count - 1), total - largest - least * (count - 1)
    while spare > 0:
        candidates = [i for i in range(1, count) if counts[i] < largest] or [i for i in range(1, count) if counts[i] < limit]
        whole, remaining = sum([portions[i] for i in candidates]), spare
        for i in candidates:
            more = min(limit - counts[i], max(1, remaining * portions[i] // whole), spare)
            counts[i] = counts[i] + more
            spare = spare - more
    return np.array(counts)


def scatter_about(own_key, extent, scale, bound, shards=(), kind=jnp.bfloat16):
    level = block_scale(own_key, extent, shards, -0.22, 0.18) if shards else 1.0
    entries = jax.random.normal(own_key, extent, jnp.float32) * scale * level
    return jnp.minimum(jnp.maximum(entries, -bound), bound).astype(kind)


def setup_inputs(seed: int = 0) -> dict:
    key_list = jax.random.split(jax.random.key(seed), 7)
    docs = scatter_about(key_list[0], (TOTAL_DOCS, BLOCK, D), 1.0, 6.0, ((0, 128),))
    routes_keys = jax.random.split(jax.random.fold_in(key_list[1], 1), TOTAL_DOCS // DOCS)
    routes_turns = jax.random.permutation(jax.random.fold_in(key_list[1], 3), TOTAL_DOCS // DOCS)
    routes = jax.vmap(lambda own, number: assign_block(jax.random.fold_in(key_list[1], 2), own, number, DOCS, PATHS, 1, CAP, 2))(routes_keys, routes_turns).reshape((TOTAL_DOCS, 1))
    level_one = scatter_about(key_list[2], (N_ROW, D, D), 1.0, 6.0, ((0, 8), (1, 16)), jnp.float32)
    level_two = scatter_about(key_list[3], (N_COL, D, D), 1.0, 6.0, ((0, 16), (1, 8)), jnp.float32)
    moment_one = scatter_about(key_list[4], (N_ROW, D, D), 3.0, 18.0, ((0, 8), (1, 16)), jnp.float32)
    moment_two = scatter_about(key_list[5], (N_COL, D, D), 3.0, 18.0, ((0, 16), (1, 8)), jnp.float32)
    return {"docs": docs, "routes": routes, "level_one": level_one, "level_two": level_two, "moment_one": moment_one, "moment_two": moment_two}


inner_rate = 64.0
outer_rate = 0.7
momentum_decay = 0.9

def normalize(values):
    return values * lax.rsqrt(lax.optimization_barrier(jnp.mean(values * values, axis=-1, keepdims=True)) + 1e-06)

def path_loss(weights, inputs, targets, row_weights):
    first, second = weights
    factor = inputs.shape[-1] ** (-0.5)
    hidden_in = jnp.dot(normalize(inputs).astype(jnp.bfloat16), first.astype(jnp.bfloat16), preferred_element_type=jnp.float32) * factor
    hidden = inputs + jax.nn.silu(hidden_in)
    output = hidden + jnp.dot(normalize(hidden).astype(jnp.bfloat16), second.astype(jnp.bfloat16), preferred_element_type=jnp.float32) * factor
    error = output - targets
    return 0.5 * jnp.sum(row_weights[:, None] * error * error) / jnp.sum(row_weights)

def train_path(first, second, rows, valid):
    width = rows.shape[-1]
    length = rows.shape[-2]
    blocks = rows.reshape(-1, length, width).astype(jnp.float32)
    inputs = blocks[:, :-1].reshape(-1, width)
    targets = blocks[:, 1:].reshape(-1, width)
    row_weights = jnp.repeat(valid.reshape(-1).astype(jnp.float32), length - 1)
    for turn in range(STEPS):
        grads = jax.grad(path_loss)((first, second), inputs, targets, row_weights)
        first = first - inner_rate * grads[0]
        second = second - inner_rate * grads[1]
    return (first, second)

def reference(docs, routes, level_one, level_two, moment_one, moment_two):
    paths = N_ROW * N_COL
    dest = routes[:, 0]
    source_routes = dest.reshape(paths, DOCS)
    onehot = (source_routes[:, :, None] == jnp.arange(paths, dtype=jnp.int32)[None, None, :]).astype(jnp.int32)
    rank = lax.optimization_barrier(jnp.sum(jnp.cumsum(onehot, axis=1) * onehot, axis=2)) - 1
    slot_all = (jnp.arange(paths, dtype=jnp.int32)[:, None] * CAP + rank).reshape(-1).astype(jnp.int32)

    def one_path(carry, path):
        sum_one, sum_two = carry
        place = jnp.where(dest == path, slot_all, paths * CAP).astype(jnp.int32)
        buffer = jnp.zeros((paths * CAP + 1, BLOCK, D), jnp.bfloat16).at[place].add(docs)[:-1]
        valid = jnp.zeros((paths * CAP + 1,), jnp.float32).at[place].add(1.0)[:-1]
        index_one = path // N_COL
        index_two = path % N_COL
        start_one = level_one[index_one]
        start_two = level_two[index_two]
        end_one, end_two = train_path(start_one, start_two, buffer, valid)
        sum_one = sum_one.at[index_one].add(start_one - end_one)
        sum_two = sum_two.at[index_two].add(start_two - end_two)
        return ((sum_one, sum_two), None)
    init = (jnp.zeros((N_ROW, D, D), jnp.float32), jnp.zeros((N_COL, D, D), jnp.float32))
    (sum_one, sum_two), unused = lax.scan(one_path, init, jnp.arange(paths, dtype=jnp.int32))
    delta_one = sum_one / N_COL
    delta_two = sum_two / N_ROW
    next_moment_one = momentum_decay * moment_one + delta_one
    next_moment_two = momentum_decay * moment_two + delta_two
    new_one = level_one - outer_rate * (delta_one + momentum_decay * next_moment_one)
    new_two = level_two - outer_rate * (delta_two + momentum_decay * next_moment_two)
    return (new_one, new_two, next_moment_one, next_moment_two)
```

```python
import functools

import jax
import jax.numpy as jnp
from jax import lax
from jax.experimental import pallas as pl
from jax.experimental.pallas import tpu as pltpu
from jax.sharding import PartitionSpec as P

STEPS = 3
inner_rate = 64.0
outer_rate = 0.7
momentum_decay = 0.9
EMPTY = 16.0
CAPACITY = 2

f32, bf16 = jnp.float32, jnp.bfloat16


def dispatch_kernel(length, routes_ref, docs_ref, out_ref):
    count = routes_ref.shape[1]
    rows = out_ref.shape[0]
    per = length * CAPACITY
    route = jnp.broadcast_to(routes_ref[...].astype(f32), (count, count))
    turned = route.T
    i = lax.broadcasted_iota(jnp.int32, (count, count), 0)
    j = lax.broadcasted_iota(jnp.int32, (count, count), 1)
    earlier = jnp.where((route == turned) & (i < j), 1.0, 0.0)
    rank = jnp.sum(earlier, axis=0, keepdims=True)
    key = (routes_ref[...].astype(f32) * per + rank).astype(jnp.int32)
    keys = jnp.concatenate([key + CAPACITY * t for t in range(length)], axis=1)
    step = 256
    for b in range(rows // step):
        at = lax.broadcasted_iota(jnp.int32, (step, length * count), 0) + b * step
        hot = jnp.where(at == keys, 1.0, 0.0)
        filled = jnp.sum(hot, axis=1, keepdims=True)
        moved = jnp.dot(hot.astype(bf16), docs_ref[...], preferred_element_type=f32)
        out_ref[b * step : (b + 1) * step, :] = (moved + EMPTY * (1.0 - filled)).astype(bf16)


def dispatch(routes, docs):
    count, length, width = docs.shape
    paths = count
    planes = jnp.transpose(docs, (1, 0, 2)).reshape(length * count, width)
    rows = 128 * length * CAPACITY
    return pl.pallas_call(
        functools.partial(dispatch_kernel, length),
        out_shape=jax.ShapeDtypeStruct((rows, width), bf16),
        in_specs=[pl.BlockSpec(memory_space=pltpu.VMEM)] * 2,
        out_specs=pl.BlockSpec(memory_space=pltpu.VMEM),
        compiler_params=pltpu.CompilerParams(vmem_limit_bytes=24 << 20),
        name="dispatch",
    )(routes.reshape(1, count), planes)


BLOCK_ROWS = 256
CHUNK = 32


def train_kernel(
    recv_ref, one_ref, two_ref, ch1_ref, ch2_ref,
    xb, a_ref, gram, z_ref, hn_ref, h_ref, sp_ref, r_ref, y_ref, ef_ref, eb_ref, g_ref, sum_ref, u2_ref, w2_ref,
):
    width = recv_ref.shape[1]
    total = recv_ref.shape[0]
    slots = total // 4
    rows = 3 * slots
    c = width**-0.5
    blocks = rows // BLOCK_ROWS
    i = lax.broadcasted_iota(jnp.int32, (128, 128), 0)
    j = lax.broadcasted_iota(jnp.int32, (128, 128), 1)
    source = ((i % 32) // 2) * 8 + (i // 32) * 2 + i % 2
    perm = jnp.where(j == source, 1.0, 0.0).astype(bf16)
    empties = jnp.zeros((1, 128), f32)
    for b in range(total // 128):
        v = recv_ref[b * 128 : (b + 1) * 128, :].astype(f32)
        gone = v > 7.0
        empties = empties + jnp.sum(jnp.where(gone[:, :128], 1.0, 0.0), axis=0, keepdims=True)
        v = jnp.where(gone, 0.0, v).astype(bf16)
        p = jnp.dot(perm, v, preferred_element_type=f32).astype(bf16)
        for t in range(4):
            xb[t * slots + b * 32 : t * slots + (b + 1) * 32, :] = p[t * 32 : (t + 1) * 32, :]
    valid = slots - jnp.max(empties, axis=1, keepdims=True) * 0.25
    inv = 1.0 / (3.0 * valid)
    k = inner_rate * c * inv

    def chunks(b, size=CHUNK):
        for q in range(BLOCK_ROWS // size):
            at = b * BLOCK_ROWS + q * size
            yield slice(at, at + size)

    for b in range(blocks):
        for s in chunks(b):
            x = xb[s, :].astype(f32)
            r = lax.rsqrt(jnp.sum(x * x, axis=1, keepdims=True) * (1.0 / width) + 1e-6)
            a_ref[s, :] = (x * r).astype(bf16)

    def block(b):
        return slice(b * BLOCK_ROWS, (b + 1) * BLOCK_ROWS)

    for b in range(blocks):
        z_ref[block(b), :] = jnp.dot(a_ref[block(b), :], one_ref[...], preferred_element_type=f32)
    for b in range(blocks):
        gram[block(b), :] = lax.dot_general(
            a_ref[block(b), :], a_ref[...], (((1,), (1,)), ((), ())), preferred_element_type=f32
        ).astype(bf16)

    def hidden(s, step):
        if step == 0:
            z = z_ref[s, :] * c
        else:
            z = z_ref[s, :] - y_ref[s, :]
        if step < STEPS - 1:
            z_ref[s, :] = z
        sg = 0.5 * jnp.tanh(0.5 * z) + 0.5
        si = z * sg
        h = xb[s, :].astype(f32) + si
        sp_ref[s, :] = (sg + si * (1.0 - sg)) * c
        r = lax.rsqrt(jnp.sum(h * h, axis=1, keepdims=True) * (1.0 / width) + 1e-6)
        h_ref[s, :] = h
        r_ref[s, :] = jnp.broadcast_to(r, (h.shape[0], 128))
        hn_ref[s, :] = (h * r).astype(bf16)

    def error(s):
        t = xb[s.start + slots : s.stop + slots, :].astype(f32)
        ef = (h_ref[s, :] + c * y_ref[s, :] - t) * k
        ef_ref[s, :] = ef
        eb_ref[s, :] = ef.astype(bf16)

    def back(s, step):
        q, h, r = y_ref[s, :], h_ref[s, :], r_ref[s, :1]
        qh = jnp.sum(q * h, axis=1, keepdims=True)
        m = (c / width) * r * r * r * qh
        g = sp_ref[s, :] * (ef_ref[s, :] + (c * r) * q - m * h)
        if step == 0:
            sum_ref[s, :] = g
        else:
            g_sum = sum_ref[s, :] + g
            sum_ref[s, :] = g_sum
        if step == STEPS - 1:
            g_ref[s, :] = g_sum.astype(bf16)
        else:
            g_ref[s, :] = g.astype(bf16)

    w2 = two_ref
    for step in range(STEPS):
        for b in range(blocks):
            for s in chunks(b):
                hidden(s, step)
            y_ref[block(b), :] = jnp.dot(hn_ref[block(b), :], w2[...], preferred_element_type=f32)
        for b in range(blocks):
            for s in chunks(b):
                error(s)
            y_ref[block(b), :] = lax.dot_general(
                eb_ref[block(b), :], w2[...], (((1,), (1,)), ((), ())), preferred_element_type=f32
            )
        for q in range(width // 128):
            s = slice(q * 128, (q + 1) * 128)
            d2 = lax.dot_general(
                hn_ref[:, s], eb_ref[...], (((0,), (0,)), ((), ())), preferred_element_type=f32
            )
            u2 = d2 if step == 0 else u2_ref[s, :] + d2
            if step < STEPS - 1:
                u2_ref[s, :] = u2
            else:
                ch2_ref[s, :] = u2.astype(bf16)
        for b in range(blocks):
            for s in chunks(b):
                back(s, step)
        if step < STEPS - 1:
            for q in range(width // 128):
                s = slice(q * 128, (q + 1) * 128)
                w2_ref[s, :] = (two_ref[s, :].astype(f32) - u2_ref[s, :]).astype(bf16)
            w2 = w2_ref
            for b in range(blocks):
                y_ref[block(b), :] = jnp.dot(gram[block(b), :], g_ref[...], preferred_element_type=f32)
    for q in range(width // 128):
        s = slice(q * 128, (q + 1) * 128)
        d1 = lax.dot_general(a_ref[:, s], g_ref[...], (((0,), (0,)), ((), ())), preferred_element_type=f32)
        ch1_ref[s, :] = (d1 * (1.0 / c)).astype(bf16)


def train(recv, one, two):
    total, width = recv.shape
    rows = total // 4 * 3
    vm = lambda *shape, t=f32: pltpu.VMEM(shape, t)
    return pl.pallas_call(
        train_kernel,
        out_shape=[jax.ShapeDtypeStruct((width, width), bf16)] * 2,
        in_specs=[pl.BlockSpec(memory_space=pltpu.VMEM)] * 3,
        out_specs=[pl.BlockSpec(memory_space=pltpu.VMEM)] * 2,
        scratch_shapes=[
            vm(total, width, t=bf16),
            vm(rows, width, t=bf16),
            vm(rows, rows, t=bf16),
            vm(rows, width),
            vm(rows, width, t=bf16),
            vm(rows, width),
            vm(rows, width),
            vm(rows, 128),
            vm(rows, width),
            vm(rows, width),
            vm(rows, width, t=bf16),
            vm(rows, width, t=bf16),
            vm(rows, width),
            vm(width, width),
            vm(width, width, t=bf16),
        ],
        compiler_params=pltpu.CompilerParams(vmem_limit_bytes=56 << 20),
        name="train",
    )(recv, one, two)


def a2a(array, axis):
    return lax.all_to_all(array, axis, 0, 0, tiled=True)


def shards(docs, routes, level_one, level_two, moment_one, moment_two):
    n_row = lax.axis_size("row")
    n_col = lax.axis_size("col")
    count, length, width = docs.shape
    own_one = level_one.astype(bf16)
    own_two = level_two.astype(bf16)
    whole_two = a2a(jnp.broadcast_to(own_two, (n_row, *own_two.shape[1:])), "row").reshape(width, width)
    whole_one = a2a(jnp.broadcast_to(own_one, (n_col, *own_one.shape[1:])), "col").reshape(width, width)
    outgoing = dispatch(routes, docs)
    recv = a2a(outgoing.reshape(n_row * n_col, length * CAPACITY, width), ("row", "col"))
    change_one, change_two = train(recv.reshape(-1, width), whole_one, whole_two)
    got_two = a2a(change_two.reshape(n_row, -1, width), "row")
    got_one = a2a(change_one.reshape(n_col, -1, width), "col")
    delta_one = (jnp.sum(got_one.astype(f32), axis=0) / n_col)[None]
    delta_two = (jnp.sum(got_two.astype(f32), axis=0) / n_row)[None]
    next_moment_one = momentum_decay * moment_one + delta_one
    next_moment_two = momentum_decay * moment_two + delta_two
    new_one = level_one - outer_rate * (delta_one + momentum_decay * next_moment_one)
    new_two = level_two - outer_rate * (delta_two + momentum_decay * next_moment_two)
    return (new_one, new_two, next_moment_one, next_moment_two)


def solution(mesh):
    placed = (
        P(("row", "col"), None, None),
        P(("row", "col"), None),
        P("row", "col", None),
        P("col", "row", None),
        P("row", "col", None),
        P("col", "row", None),
    )
    return jax.shard_map(
        shards,
        mesh=mesh,
        in_specs=placed,
        out_specs=(
            P("row", "col", None),
            P("col", "row", None),
            P("row", "col", None),
            P("col", "row", None),
        ),
        check_vma=False,
    )
```

```python
import functools

import jax
import jax.numpy as jnp
from jax import lax
from jax.experimental import pallas as pl
from jax.experimental.pallas import tpu as pltpu
from jax.sharding import PartitionSpec as P

STEPS = 3
inner_rate = 64.0
outer_rate = 0.7
momentum_decay = 0.9
EMPTY = 16.0
CAPACITY = 2

f32, bf16 = jnp.float32, jnp.bfloat16


def dispatch_kernel(length, routes_ref, docs_ref, out_ref):
    count = routes_ref.shape[1]
    rows = out_ref.shape[0]
    per = length * CAPACITY
    route = jnp.broadcast_to(routes_ref[...].astype(f32), (count, count))
    turned = route.T
    i = lax.broadcasted_iota(jnp.int32, (count, count), 0)
    j = lax.broadcasted_iota(jnp.int32, (count, count), 1)
    earlier = jnp.where((route == turned) & (i < j), 1.0, 0.0)
    rank = jnp.sum(earlier, axis=0, keepdims=True)
    key = (routes_ref[...].astype(f32) * per + rank).astype(jnp.int32)
    keys = jnp.concatenate([key + CAPACITY * t for t in range(length)], axis=1)
    step = 256
    for b in range(rows // step):
        at = lax.broadcasted_iota(jnp.int32, (step, length * count), 0) + b * step
        hot = jnp.where(at == keys, 1.0, 0.0)
        filled = jnp.sum(hot, axis=1, keepdims=True)
        moved = jnp.dot(hot.astype(bf16), docs_ref[...], preferred_element_type=f32)
        out_ref[b * step : (b + 1) * step, :] = (moved + EMPTY * (1.0 - filled)).astype(bf16)


def cost(flops, moved):
    return pl.CostEstimate(flops=flops, transcendentals=0, bytes_accessed=moved)


def dispatch(routes, docs):
    count, length, width = docs.shape
    paths = count
    planes = jnp.transpose(docs, (1, 0, 2)).reshape(length * count, width)
    rows = 128 * length * CAPACITY
    return pl.pallas_call(
        functools.partial(dispatch_kernel, length),
        out_shape=jax.ShapeDtypeStruct((rows, width), bf16),
        in_specs=[pl.BlockSpec(memory_space=pltpu.VMEM)] * 2,
        out_specs=pl.BlockSpec(memory_space=pltpu.VMEM),
        compiler_params=pltpu.CompilerParams(vmem_limit_bytes=24 << 20),
        cost_estimate=cost(2 * rows * length * count * width, 4 * rows * width),
        name="dispatch",
    )(routes.reshape(1, count), planes)


BLOCK_ROWS = 256
CHUNK = 32
TRAIN_VMEM = 24 << 20
TAIL_VMEM = 10 << 20


def train_kernel(
    recv_ref, one_ref, two_ref,
    ch2_ref, a_ref, h_ref, sp_ref, r_ref, ef_ref, eb_ref, sum_ref, w2_ref,
    xb, gram, z_ref, hn_ref, y_ref, g_ref, u2_ref,
):
    width = recv_ref.shape[1]
    total = recv_ref.shape[0]
    slots = total // 4
    rows = 3 * slots
    c = width**-0.5
    blocks = rows // BLOCK_ROWS
    i = lax.broadcasted_iota(jnp.int32, (128, 128), 0)
    j = lax.broadcasted_iota(jnp.int32, (128, 128), 1)
    source = ((i % 32) // 2) * 8 + (i // 32) * 2 + i % 2
    perm = jnp.where(j == source, 1.0, 0.0).astype(bf16)
    empties = jnp.zeros((1, 128), f32)
    for b in range(total // 128):
        v = recv_ref[b * 128 : (b + 1) * 128, :].astype(f32)
        gone = v > 7.0
        empties = empties + jnp.sum(jnp.where(gone[:, :128], 1.0, 0.0), axis=0, keepdims=True)
        v = jnp.where(gone, 0.0, v).astype(bf16)
        p = jnp.dot(perm, v, preferred_element_type=f32).astype(bf16)
        for t in range(4):
            xb[t * slots + b * 32 : t * slots + (b + 1) * 32, :] = p[t * 32 : (t + 1) * 32, :]
    valid = slots - jnp.max(empties, axis=1, keepdims=True) * 0.25
    inv = 1.0 / (3.0 * valid)
    k = inner_rate * c * inv

    def chunks(b, size=CHUNK):
        for q in range(BLOCK_ROWS // size):
            at = b * BLOCK_ROWS + q * size
            yield slice(at, at + size)

    for b in range(blocks):
        for s in chunks(b):
            x = xb[s, :].astype(f32)
            r = lax.rsqrt(jnp.sum(x * x, axis=1, keepdims=True) * (1.0 / width) + 1e-6)
            a_ref[s, :] = (x * r).astype(bf16)

    def block(b):
        return slice(b * BLOCK_ROWS, (b + 1) * BLOCK_ROWS)

    for b in range(blocks):
        z_ref[block(b), :] = jnp.dot(a_ref[block(b), :], one_ref[...], preferred_element_type=f32)
    for b in range(blocks):
        gram[block(b), :] = lax.dot_general(
            a_ref[block(b), :], a_ref[...], (((1,), (1,)), ((), ())), preferred_element_type=f32
        ).astype(bf16)

    def hidden(s, step):
        if step == 0:
            z = z_ref[s, :] * c
        else:
            z = z_ref[s, :] - y_ref[s, :]
        if step < STEPS - 1:
            z_ref[s, :] = z
        sg = 0.5 * jnp.tanh(0.5 * z) + 0.5
        si = z * sg
        h = xb[s, :].astype(f32) + si
        sp_ref[s, :] = (sg + si * (1.0 - sg)) * c
        r = lax.rsqrt(jnp.sum(h * h, axis=1, keepdims=True) * (1.0 / width) + 1e-6)
        h_ref[s, :] = h
        r_ref[s, :] = jnp.broadcast_to(r, (h.shape[0], 128))
        hn_ref[s, :] = (h * r).astype(bf16)

    def error(s):
        t = xb[s.start + slots : s.stop + slots, :].astype(f32)
        ef = (h_ref[s, :] + c * y_ref[s, :] - t) * k
        ef_ref[s, :] = ef
        eb_ref[s, :] = ef.astype(bf16)

    def back(s, step):
        g = slope(s, y_ref, h_ref, sp_ref, r_ref, ef_ref)
        if step == 0:
            sum_ref[s, :] = g
        else:
            sum_ref[s, :] = sum_ref[s, :] + g
        g_ref[s, :] = g.astype(bf16)

    w2 = two_ref
    for step in range(STEPS):
        for b in range(blocks):
            for s in chunks(b):
                hidden(s, step)
            y_ref[block(b), :] = jnp.dot(hn_ref[block(b), :], w2[...], preferred_element_type=f32)
        for b in range(blocks):
            for s in chunks(b):
                error(s)
            if step < STEPS - 1:
                y_ref[block(b), :] = lax.dot_general(
                    eb_ref[block(b), :], w2[...], (((1,), (1,)), ((), ())), preferred_element_type=f32
                )
        for q in range(width // 128):
            s = slice(q * 128, (q + 1) * 128)
            d2 = lax.dot_general(
                hn_ref[:, s], eb_ref[...], (((0,), (0,)), ((), ())), preferred_element_type=f32
            )
            u2 = d2 if step == 0 else u2_ref[s, :] + d2
            if step < STEPS - 1:
                u2_ref[s, :] = u2
            else:
                ch2_ref[s, :] = u2.astype(bf16)
        if step < STEPS - 1:
            for b in range(blocks):
                for s in chunks(b):
                    back(s, step)
            for q in range(width // 128):
                s = slice(q * 128, (q + 1) * 128)
                w2_ref[s, :] = (two_ref[s, :].astype(f32) - u2_ref[s, :]).astype(bf16)
            w2 = w2_ref
            for b in range(blocks):
                y_ref[block(b), :] = jnp.dot(gram[block(b), :], g_ref[...], preferred_element_type=f32)


def slope(s, y_ref, h_ref, sp_ref, r_ref, ef_ref):
    width = h_ref.shape[1]
    c = width**-0.5
    q, h, r = y_ref[s, :], h_ref[s, :], r_ref[s, :1]
    qh = jnp.sum(q * h, axis=1, keepdims=True)
    m = (c / width) * r * r * r * qh
    return sp_ref[s, :] * (ef_ref[s, :] + (c * r) * q - m * h)


def tail_kernel(a_ref, h_ref, sp_ref, r_ref, ef_ref, eb_ref, sum_ref, w2_ref, ch1_ref, y_ref, g_ref):
    rows, width = h_ref.shape
    for b in range(rows // BLOCK_ROWS):
        at = slice(b * BLOCK_ROWS, (b + 1) * BLOCK_ROWS)
        y_ref[at, :] = lax.dot_general(
            eb_ref[at, :], w2_ref[...], (((1,), (1,)), ((), ())), preferred_element_type=f32
        )
    for q in range(rows // CHUNK):
        s = slice(q * CHUNK, (q + 1) * CHUNK)
        g_ref[s, :] = (sum_ref[s, :] + slope(s, y_ref, h_ref, sp_ref, r_ref, ef_ref)).astype(bf16)
    for q in range(width // 128):
        s = slice(q * 128, (q + 1) * 128)
        d1 = lax.dot_general(a_ref[:, s], g_ref[...], (((0,), (0,)), ((), ())), preferred_element_type=f32)
        ch1_ref[s, :] = (d1 * (width**0.5)).astype(bf16)


def train(recv, one, two):
    total, width = recv.shape
    rows = total // 4 * 3
    vm = lambda *shape, t=f32: pltpu.VMEM(shape, t)
    like = lambda *shape, t=f32: jax.ShapeDtypeStruct(shape, t)
    spec = pl.BlockSpec(memory_space=pltpu.VMEM)
    change_two, *kept = pl.pallas_call(
        train_kernel,
        out_shape=[
            like(width, width, t=bf16),
            like(rows, width, t=bf16),
            like(rows, width),
            like(rows, width),
            like(rows, 128),
            like(rows, width),
            like(rows, width, t=bf16),
            like(rows, width),
            like(width, width, t=bf16),
        ],
        in_specs=[spec] * 3,
        out_specs=[spec] * 9,
        scratch_shapes=[
            vm(total, width, t=bf16),
            vm(rows, rows, t=bf16),
            vm(rows, width),
            vm(rows, width, t=bf16),
            vm(rows, width),
            vm(rows, width, t=bf16),
            vm(width, width),
        ],
        compiler_params=pltpu.CompilerParams(vmem_limit_bytes=TRAIN_VMEM),
        cost_estimate=cost(14 * 2 * rows * width * width, 30 * rows * width),
        name="train",
    )(recv, one, two)
    change_one = pl.pallas_call(
        tail_kernel,
        out_shape=like(width, width, t=bf16),
        in_specs=[spec] * 8,
        out_specs=spec,
        scratch_shapes=[vm(rows, width), vm(rows, width, t=bf16)],
        compiler_params=pltpu.CompilerParams(vmem_limit_bytes=TAIL_VMEM),
        cost_estimate=cost(2 * 2 * rows * width * width, 30 * rows * width),
        name="tail",
    )(*kept)
    return change_one, change_two


def a2a(array, axis):
    return lax.all_to_all(array, axis, 0, 0, tiled=True)


def swap(array, bit):
    n = lax.axis_size("col")
    return lax.ppermute(array, "col", [(i, i ^ bit) for i in range(n)])


Z_BIT, Y_BITS, CORE_BIT = 8, (2, 4, 6), 1


def assemble_kernel(places_ref, near_ref, far_ref, out_ref, sems):
    n = near_ref.shape[0]
    copies = []
    for k in range(n):
        copies.append(pltpu.make_async_copy(near_ref.at[k], out_ref.at[places_ref[k]], sems.at[k]))
        copies.append(pltpu.make_async_copy(far_ref.at[k], out_ref.at[places_ref[n + k]], sems.at[n + k]))
    for copy in copies:
        copy.start()
    for copy in copies:
        copy.wait()


def gather_near(own):
    pair = jnp.stack([own, swap(own, Z_BIT)])
    return jnp.concatenate([pair, *(swap(pair, bit) for bit in Y_BITS)])


def gather_far(near):
    me = lax.axis_index("col")
    far = swap(near, CORE_BIT)
    order = jnp.array([y | z for y in (0, *Y_BITS) for z in (0, Z_BIT)], jnp.int32)
    places = jnp.concatenate([me ^ order, me ^ order ^ CORE_BIT])
    n = 2 * near.shape[0]
    return pl.pallas_call(
        assemble_kernel,
        out_shape=jax.ShapeDtypeStruct((n, *near.shape[1:]), near.dtype),
        in_specs=[pl.BlockSpec(memory_space=pltpu.SMEM)] + [pl.BlockSpec(memory_space=pl.ANY)] * 2,
        out_specs=pl.BlockSpec(memory_space=pl.ANY),
        scratch_shapes=[pltpu.SemaphoreType.DMA((n,))],
        cost_estimate=cost(0, 2 * n * near.shape[1] * near.shape[2] * 2),
        name="assemble",
    )(places, near, far)


def pick(array, at, axis):
    return lax.dynamic_index_in_dim(array, at, axis, keepdims=False)


def reduce_one(change):
    me = lax.axis_index("col")
    me = me.astype(jnp.uint32)
    z, y, core = me >> 3, (me >> 1) & 3, me & 1
    width = change.shape[1]
    tiles = change.reshape(2, 4, 2, -1, width)
    got = swap(pick(tiles, core ^ 1, 2), CORE_BIT)
    part = (pick(tiles, core, 2).astype(f32) + got.astype(f32)).astype(bf16)
    got = [swap(pick(part, y ^ jnp.uint32(bit // 2), 1), bit) for bit in Y_BITS]
    part = pick(part, y, 1).astype(f32)
    for g in got:
        part = part + g.astype(f32)
    part = part.astype(bf16)
    got = swap(pick(part, z ^ 1, 0), Z_BIT)
    return pick(part, z, 0).astype(f32) + got.astype(f32)


def shards(docs, routes, level_one, level_two, moment_one, moment_two):
    n_row = lax.axis_size("row")
    n_col = lax.axis_size("col")
    count, length, width = docs.shape
    own_one = level_one.astype(bf16)
    own_two = level_two.astype(bf16)
    whole_two = a2a(jnp.broadcast_to(own_two, (n_row, *own_two.shape[1:])), "row").reshape(width, width)
    near = gather_near(own_one[0])
    outgoing = dispatch(routes, docs)
    near, outgoing = lax.optimization_barrier((near, outgoing))
    whole_one = gather_far(near).reshape(width, width)
    recv = a2a(outgoing.reshape(n_row * n_col, length * CAPACITY, width), ("row", "col"))
    change_one, change_two = train(recv.reshape(-1, width), whole_one, whole_two)
    got_two = a2a(change_two.reshape(n_row, -1, width), "row")
    delta_one = (reduce_one(change_one) / n_col)[None]
    delta_two = (jnp.sum(got_two.astype(f32), axis=0) / n_row)[None]
    next_moment_one = momentum_decay * moment_one + delta_one
    next_moment_two = momentum_decay * moment_two + delta_two
    new_one = level_one - outer_rate * (delta_one + momentum_decay * next_moment_one)
    new_two = level_two - outer_rate * (delta_two + momentum_decay * next_moment_two)
    return (new_one, new_two, next_moment_one, next_moment_two)


def solution(mesh):
    placed = (
        P(("row", "col"), None, None),
        P(("row", "col"), None),
        P("row", "col", None),
        P("col", "row", None),
        P("row", "col", None),
        P("col", "row", None),
    )
    return jax.shard_map(
        shards,
        mesh=mesh,
        in_specs=placed,
        out_specs=(
            P("row", "col", None),
            P("col", "row", None),
            P("row", "col", None),
            P("col", "row", None),
        ),
        check_vma=False,
    )
```

```python
import functools

import jax
import jax.numpy as jnp
from jax import lax
from jax.experimental import pallas as pl
from jax.experimental.pallas import tpu as pltpu
from jax.sharding import PartitionSpec as P

STEPS = 3
inner_rate = 64.0
outer_rate = 0.7
momentum_decay = 0.9
EMPTY = 16.0
CAPACITY = 2

f32, bf16 = jnp.float32, jnp.bfloat16


def dispatch_kernel(length, routes_ref, docs_ref, out_ref):
    count = routes_ref.shape[1]
    rows = out_ref.shape[0]
    per = length * CAPACITY
    route = jnp.broadcast_to(routes_ref[...].astype(f32), (count, count))
    turned = route.T
    i = lax.broadcasted_iota(jnp.int32, (count, count), 0)
    j = lax.broadcasted_iota(jnp.int32, (count, count), 1)
    earlier = jnp.where((route == turned) & (i < j), 1.0, 0.0)
    rank = jnp.sum(earlier, axis=0, keepdims=True)
    key = (routes_ref[...].astype(f32) * per + rank).astype(jnp.int32)
    keys = jnp.concatenate([key + CAPACITY * t for t in range(length)], axis=1)
    step = 256
    for b in range(rows // step):
        at = lax.broadcasted_iota(jnp.int32, (step, length * count), 0) + b * step
        hot = jnp.where(at == keys, 1.0, 0.0)
        filled = jnp.sum(hot, axis=1, keepdims=True)
        moved = jnp.dot(hot.astype(bf16), docs_ref[...], preferred_element_type=f32)
        out_ref[b * step : (b + 1) * step, :] = (moved + EMPTY * (1.0 - filled)).astype(bf16)


def cost(flops, moved):
    return pl.CostEstimate(flops=flops, transcendentals=0, bytes_accessed=moved)


def dispatch(routes, docs):
    count, length, width = docs.shape
    paths = count
    planes = jnp.transpose(docs, (1, 0, 2)).reshape(length * count, width)
    rows = 128 * length * CAPACITY
    return pl.pallas_call(
        functools.partial(dispatch_kernel, length),
        out_shape=jax.ShapeDtypeStruct((rows, width), bf16),
        in_specs=[pl.BlockSpec(memory_space=pltpu.VMEM)] * 2,
        out_specs=pl.BlockSpec(memory_space=pltpu.VMEM),
        compiler_params=pltpu.CompilerParams(vmem_limit_bytes=24 << 20),
        cost_estimate=cost(2 * rows * length * count * width, 4 * rows * width),
        name="dispatch",
    )(routes.reshape(1, count), planes)


BLOCK_ROWS = 256
CHUNK = 32
TRAIN_VMEM = 24 << 20
TAIL_VMEM = 10 << 20


def train_kernel(
    recv_ref, one_ref, two_ref,
    ch2_ref, a_ref, h_ref, sp_ref, r_ref, ef_ref, eb_ref, sum_ref, w2_ref,
    xb, gram, z_ref, hn_ref, y_ref, g_ref, u2_ref,
):
    width = recv_ref.shape[1]
    total = recv_ref.shape[0]
    slots = total // 4
    rows = 3 * slots
    c = width**-0.5
    blocks = rows // BLOCK_ROWS
    i = lax.broadcasted_iota(jnp.int32, (128, 128), 0)
    j = lax.broadcasted_iota(jnp.int32, (128, 128), 1)
    source = ((i % 32) // 2) * 8 + (i // 32) * 2 + i % 2
    perm = jnp.where(j == source, 1.0, 0.0).astype(bf16)
    empties = jnp.zeros((1, 128), f32)
    for b in range(total // 128):
        v = recv_ref[b * 128 : (b + 1) * 128, :].astype(f32)
        gone = v > 7.0
        empties = empties + jnp.sum(jnp.where(gone[:, :128], 1.0, 0.0), axis=0, keepdims=True)
        v = jnp.where(gone, 0.0, v).astype(bf16)
        p = jnp.dot(perm, v, preferred_element_type=f32).astype(bf16)
        for t in range(4):
            xb[t * slots + b * 32 : t * slots + (b + 1) * 32, :] = p[t * 32 : (t + 1) * 32, :]
    valid = slots - jnp.max(empties, axis=1, keepdims=True) * 0.25
    inv = 1.0 / (3.0 * valid)
    k = inner_rate * c * inv

    def chunks(b, size=CHUNK):
        for q in range(BLOCK_ROWS // size):
            at = b * BLOCK_ROWS + q * size
            yield slice(at, at + size)

    for b in range(blocks):
        for s in chunks(b):
            x = xb[s, :].astype(f32)
            r = lax.rsqrt(jnp.sum(x * x, axis=1, keepdims=True) * (1.0 / width) + 1e-6)
            a_ref[s, :] = (x * r).astype(bf16)

    def block(b):
        return slice(b * BLOCK_ROWS, (b + 1) * BLOCK_ROWS)

    for b in range(blocks):
        z_ref[block(b), :] = jnp.dot(a_ref[block(b), :], one_ref[...], preferred_element_type=f32)
    for b in range(blocks):
        gram[block(b), :] = lax.dot_general(
            a_ref[block(b), :], a_ref[...], (((1,), (1,)), ((), ())), preferred_element_type=f32
        ).astype(bf16)

    def hidden(s, step):
        if step == 0:
            z = z_ref[s, :] * c
        else:
            z = z_ref[s, :] - y_ref[s, :]
        if step < STEPS - 1:
            z_ref[s, :] = z
        sg = 0.5 * jnp.tanh(0.5 * z) + 0.5
        si = z * sg
        h = xb[s, :].astype(f32) + si
        sp_ref[s, :] = (sg + si * (1.0 - sg)) * c
        r = lax.rsqrt(jnp.sum(h * h, axis=1, keepdims=True) * (1.0 / width) + 1e-6)
        h_ref[s, :] = h
        r_ref[s, :] = jnp.broadcast_to(r, (h.shape[0], 128))
        hn_ref[s, :] = (h * r).astype(bf16)

    def error(s):
        t = xb[s.start + slots : s.stop + slots, :].astype(f32)
        ef = (h_ref[s, :] + c * y_ref[s, :] - t) * k
        ef_ref[s, :] = ef
        eb_ref[s, :] = ef.astype(bf16)

    def back(s, step):
        g = slope(s, y_ref, h_ref, sp_ref, r_ref, ef_ref)
        if step == 0:
            sum_ref[s, :] = g
        else:
            sum_ref[s, :] = sum_ref[s, :] + g
        g_ref[s, :] = g.astype(bf16)

    w2 = two_ref
    for step in range(STEPS):
        for b in range(blocks):
            for s in chunks(b):
                hidden(s, step)
            y_ref[block(b), :] = jnp.dot(hn_ref[block(b), :], w2[...], preferred_element_type=f32)
        for b in range(blocks):
            for s in chunks(b):
                error(s)
            if step < STEPS - 1:
                y_ref[block(b), :] = lax.dot_general(
                    eb_ref[block(b), :], w2[...], (((1,), (1,)), ((), ())), preferred_element_type=f32
                )
        for q in range(width // 128):
            s = slice(q * 128, (q + 1) * 128)
            d2 = lax.dot_general(
                hn_ref[:, s], eb_ref[...], (((0,), (0,)), ((), ())), preferred_element_type=f32
            )
            u2 = d2 if step == 0 else u2_ref[s, :] + d2
            if step < STEPS - 1:
                u2_ref[s, :] = u2
            else:
                ch2_ref[s, :] = u2.astype(bf16)
        if step < STEPS - 1:
            for b in range(blocks):
                for s in chunks(b):
                    back(s, step)
            for q in range(width // 128):
                s = slice(q * 128, (q + 1) * 128)
                w2_ref[s, :] = (two_ref[s, :].astype(f32) - u2_ref[s, :]).astype(bf16)
            w2 = w2_ref
            for b in range(blocks):
                y_ref[block(b), :] = jnp.dot(gram[block(b), :], g_ref[...], preferred_element_type=f32)


def slope(s, y_ref, h_ref, sp_ref, r_ref, ef_ref):
    width = h_ref.shape[1]
    c = width**-0.5
    q, h, r = y_ref[s, :], h_ref[s, :], r_ref[s, :1]
    qh = jnp.sum(q * h, axis=1, keepdims=True)
    m = (c / width) * r * r * r * qh
    return sp_ref[s, :] * (ef_ref[s, :] + (c * r) * q - m * h)


def tail_kernel(a_ref, h_ref, sp_ref, r_ref, ef_ref, eb_ref, sum_ref, w2_ref, ch1_ref, y_ref, g_ref):
    rows, width = h_ref.shape
    for b in range(rows // BLOCK_ROWS):
        at = slice(b * BLOCK_ROWS, (b + 1) * BLOCK_ROWS)
        y_ref[at, :] = lax.dot_general(
            eb_ref[at, :], w2_ref[...], (((1,), (1,)), ((), ())), preferred_element_type=f32
        )
    for q in range(rows // CHUNK):
        s = slice(q * CHUNK, (q + 1) * CHUNK)
        g_ref[s, :] = (sum_ref[s, :] + slope(s, y_ref, h_ref, sp_ref, r_ref, ef_ref)).astype(bf16)
    for q in range(width // 128):
        s = slice(q * 128, (q + 1) * 128)
        d1 = lax.dot_general(a_ref[:, s], g_ref[...], (((0,), (0,)), ((), ())), preferred_element_type=f32)
        ch1_ref[s, :] = (d1 * (width**0.5)).astype(bf16)


def train(recv, one, two):
    total, width = recv.shape
    rows = total // 4 * 3
    vm = lambda *shape, t=f32: pltpu.VMEM(shape, t)
    like = lambda *shape, t=f32: jax.ShapeDtypeStruct(shape, t)
    spec = pl.BlockSpec(memory_space=pltpu.VMEM)
    change_two, *kept = pl.pallas_call(
        train_kernel,
        out_shape=[
            like(width, width, t=bf16),
            like(rows, width, t=bf16),
            like(rows, width),
            like(rows, width),
            like(rows, 128),
            like(rows, width),
            like(rows, width, t=bf16),
            like(rows, width),
            like(width, width, t=bf16),
        ],
        in_specs=[spec] * 3,
        out_specs=[spec] * 9,
        scratch_shapes=[
            vm(total, width, t=bf16),
            vm(rows, rows, t=bf16),
            vm(rows, width),
            vm(rows, width, t=bf16),
            vm(rows, width),
            vm(rows, width, t=bf16),
            vm(width, width),
        ],
        compiler_params=pltpu.CompilerParams(vmem_limit_bytes=TRAIN_VMEM),
        cost_estimate=cost(14 * 2 * rows * width * width, 30 * rows * width),
        name="train",
    )(recv, one, two)
    change_one = pl.pallas_call(
        tail_kernel,
        out_shape=like(width, width, t=bf16),
        in_specs=[spec] * 8,
        out_specs=spec,
        scratch_shapes=[vm(rows, width), vm(rows, width, t=bf16)],
        compiler_params=pltpu.CompilerParams(vmem_limit_bytes=TAIL_VMEM),
        cost_estimate=cost(2 * 2 * rows * width * width, 30 * rows * width),
        name="tail",
    )(*kept)
    return change_one, change_two


def a2a(array, axis):
    return lax.all_to_all(array, axis, 0, 0, tiled=True)


def swap(array, bit):
    n = lax.axis_size("col")
    return lax.ppermute(array, "col", [(i, i ^ bit) for i in range(n)])


Z_BIT, Y_BITS, CORE_BIT = 8, (2, 4, 6), 1


def assemble_kernel(places_ref, near_ref, far_ref, out_ref):
    n = near_ref.shape[0]
    for k in range(n):
        out_ref[places_ref[k]] = near_ref[k]
        out_ref[places_ref[n + k]] = far_ref[k]


def gather_two(own, other):
    z = lax.axis_index("row") >> 2
    pair = jnp.stack([jnp.where(z == 0, own, other), jnp.where(z == 0, other, own)])
    sent = jnp.broadcast_to(pair, (4, *pair.shape))
    groups = [[0, 1, 2, 3], [4, 5, 6, 7]]
    got = lax.all_to_all(sent, "row", 0, 0, tiled=True, axis_index_groups=groups)
    return jnp.swapaxes(got, 0, 1)


def gather_near(own, other):
    pair = jnp.stack([own, other])
    return jnp.concatenate([pair, *(swap(pair, bit) for bit in Y_BITS)])


def gather_far(near):
    me = lax.axis_index("col")
    far = swap(near, CORE_BIT)
    order = jnp.array([y | z for y in (0, *Y_BITS) for z in (0, Z_BIT)], jnp.int32)
    places = jnp.concatenate([me ^ order, me ^ order ^ CORE_BIT])
    n = 2 * near.shape[0]
    return pl.pallas_call(
        assemble_kernel,
        out_shape=jax.ShapeDtypeStruct((n, *near.shape[1:]), near.dtype),
        in_specs=[pl.BlockSpec(memory_space=pltpu.SMEM)] + [pl.BlockSpec(memory_space=pltpu.VMEM)] * 2,
        out_specs=pl.BlockSpec(memory_space=pltpu.VMEM),
        compiler_params=pltpu.CompilerParams(vmem_limit_bytes=8 << 20),
        cost_estimate=cost(0, 2 * n * near.shape[1] * near.shape[2] * 2),
        name="assemble",
    )(places, near, far)


def pick(array, at, axis):
    return lax.dynamic_index_in_dim(array, at, axis, keepdims=False)


def reduce_one(change):
    me = lax.axis_index("col")
    me = me.astype(jnp.uint32)
    z, y, core = me >> 3, (me >> 1) & 3, me & 1
    width = change.shape[1]
    tiles = change.reshape(2, 4, 2, -1, width)
    got = swap(pick(tiles, core ^ 1, 2), CORE_BIT)
    part = (pick(tiles, core, 2).astype(f32) + got.astype(f32)).astype(bf16)
    got = [swap(pick(part, y ^ jnp.uint32(bit // 2), 1), bit) for bit in Y_BITS]
    part = pick(part, y, 1).astype(f32)
    for g in got:
        part = part + g.astype(f32)
    part = part.astype(bf16)
    got = swap(pick(part, z ^ 1, 0), Z_BIT)
    return pick(part, z, 0).astype(f32) + got.astype(f32)


def shards(docs, routes, level_one, level_two, moment_one, moment_two):
    n_row = lax.axis_size("row")
    n_col = lax.axis_size("col")
    count, length, width = docs.shape
    own_one = level_one[0].astype(bf16)
    own_two = level_two[0].astype(bf16)
    other_one = swap(own_one, Z_BIT)
    other_two = lax.ppermute(own_two, "row", [(i, i ^ 4) for i in range(n_row)])
    outgoing = dispatch(routes, docs)
    other_one, other_two, outgoing = lax.optimization_barrier((other_one, other_two, outgoing))
    whole_two = gather_two(own_two, other_two).reshape(width, width)
    near = gather_near(own_one, other_one)
    near, outgoing = lax.optimization_barrier((near, outgoing))
    whole_one = gather_far(near).reshape(width, width)
    recv = a2a(outgoing.reshape(n_row * n_col, length * CAPACITY, width), ("row", "col"))
    change_one, change_two = train(recv.reshape(-1, width), whole_one, whole_two)
    got_two = a2a(change_two.reshape(n_row, -1, width), "row")
    delta_one = (reduce_one(change_one) / n_col)[None]
    delta_two = (jnp.sum(got_two.astype(f32), axis=0) / n_row)[None]
    next_moment_one = momentum_decay * moment_one + delta_one
    next_moment_two = momentum_decay * moment_two + delta_two
    new_one = level_one - outer_rate * (delta_one + momentum_decay * next_moment_one)
    new_two = level_two - outer_rate * (delta_two + momentum_decay * next_moment_two)
    return (new_one, new_two, next_moment_one, next_moment_two)


def solution(mesh):
    placed = (
        P(("row", "col"), None, None),
        P(("row", "col"), None),
        P("row", "col", None),
        P("col", "row", None),
        P("row", "col", None),
        P("col", "row", None),
    )
    return jax.shard_map(
        shards,
        mesh=mesh,
        in_specs=placed,
        out_specs=(
            P("row", "col", None),
            P("col", "row", None),
            P("row", "col", None),
            P("col", "row", None),
        ),
        check_vma=False,
    )
```

```python
import functools

import jax
import jax.numpy as jnp
from jax import lax
from jax.experimental import pallas as pl
from jax.experimental.pallas import tpu as pltpu
from jax.sharding import PartitionSpec as P

STEPS = 3
inner_rate = 64.0
outer_rate = 0.7
momentum_decay = 0.9
EMPTY = 16.0
CAPACITY = 2

f32, bf16 = jnp.float32, jnp.bfloat16


def dispatch_kernel(length, routes_ref, docs_ref, out_ref):
    count = routes_ref.shape[1]
    rows = out_ref.shape[0]
    per = length * CAPACITY
    route = jnp.broadcast_to(routes_ref[...].astype(f32), (count, count))
    turned = route.T
    i = lax.broadcasted_iota(jnp.int32, (count, count), 0)
    j = lax.broadcasted_iota(jnp.int32, (count, count), 1)
    earlier = jnp.where((route == turned) & (i < j), 1.0, 0.0)
    rank = jnp.sum(earlier, axis=0, keepdims=True)
    key = (routes_ref[...].astype(f32) * per + rank).astype(jnp.int32)
    keys = jnp.concatenate([key + CAPACITY * t for t in range(length)], axis=1)
    step = 256
    for b in range(rows // step):
        at = lax.broadcasted_iota(jnp.int32, (step, length * count), 0) + b * step
        hot = jnp.where(at == keys, 1.0, 0.0)
        filled = jnp.sum(hot, axis=1, keepdims=True)
        moved = jnp.dot(hot.astype(bf16), docs_ref[...], preferred_element_type=f32)
        out_ref[b * step : (b + 1) * step, :] = (moved + EMPTY * (1.0 - filled)).astype(bf16)


def cost(flops, moved):
    return pl.CostEstimate(flops=flops, transcendentals=0, bytes_accessed=moved)


def dispatch(routes, docs):
    count, length, width = docs.shape
    paths = count
    planes = jnp.transpose(docs, (1, 0, 2)).reshape(length * count, width)
    rows = 128 * length * CAPACITY
    return pl.pallas_call(
        functools.partial(dispatch_kernel, length),
        out_shape=jax.ShapeDtypeStruct((rows, width), bf16),
        in_specs=[pl.BlockSpec(memory_space=pltpu.VMEM)] * 2,
        out_specs=pl.BlockSpec(memory_space=pltpu.VMEM),
        compiler_params=pltpu.CompilerParams(vmem_limit_bytes=24 << 20),
        cost_estimate=cost(2 * rows * length * count * width, 4 * rows * width),
        name="dispatch",
    )(routes.reshape(1, count), planes)


BLOCK_ROWS = 256
CHUNK = 32
PREP_VMEM = 8 << 20
TRAIN_VMEM = 54 << 20


def block(b):
    return slice(b * BLOCK_ROWS, (b + 1) * BLOCK_ROWS)


def chunks(b):
    for q in range(BLOCK_ROWS // CHUNK):
        at = b * BLOCK_ROWS + q * CHUNK
        yield slice(at, at + CHUNK)


def turned_dot(a, b):
    return lax.dot_general(a, b, (((1,), (1,)), ((), ())), preferred_element_type=f32)


def hidden(s, z, xb, hn_ref, h_ref, sp_ref, r_ref):
    width = z.shape[1]
    c = width**-0.5
    sg = 0.5 * jnp.tanh(0.5 * z) + 0.5
    si = z * sg
    h = xb[s, :].astype(f32) + si
    sp_ref[s, :] = (sg + si * (1.0 - sg)) * c
    r = lax.rsqrt(jnp.sum(h * h, axis=1, keepdims=True) * (1.0 / width) + 1e-6)
    h_ref[s, :] = h
    r_ref[s, :] = jnp.broadcast_to(r, (h.shape[0], 128))
    hn_ref[s, :] = (h * r).astype(bf16)


def prepare_kernel(recv_ref, one_ref, xb, a_ref, gram, k_ref, z_ref, hn_ref, h_ref, sp_ref, r_ref):
    total, width = recv_ref.shape
    slots = total // 4
    rows = 3 * slots
    c = width**-0.5
    blocks = rows // BLOCK_ROWS
    i = lax.broadcasted_iota(jnp.int32, (128, 128), 0)
    j = lax.broadcasted_iota(jnp.int32, (128, 128), 1)
    source = ((i % 32) // 2) * 8 + (i // 32) * 2 + i % 2
    perm = jnp.where(j == source, 1.0, 0.0).astype(bf16)
    empties = jnp.zeros((1, 128), f32)
    for b in range(total // 128):
        v = recv_ref[b * 128 : (b + 1) * 128, :].astype(f32)
        gone = v > 7.0
        empties = empties + jnp.sum(jnp.where(gone[:, :128], 1.0, 0.0), axis=0, keepdims=True)
        v = jnp.where(gone, 0.0, v).astype(bf16)
        p = jnp.dot(perm, v, preferred_element_type=f32).astype(bf16)
        for t in range(4):
            xb[t * slots + b * 32 : t * slots + (b + 1) * 32, :] = p[t * 32 : (t + 1) * 32, :]
    valid = slots - empties * 0.25
    k_ref[...] = jnp.broadcast_to(inner_rate * c / (3.0 * valid), k_ref.shape)
    for b in range(blocks):
        for s in chunks(b):
            x = xb[s, :].astype(f32)
            r = lax.rsqrt(jnp.sum(x * x, axis=1, keepdims=True) * (1.0 / width) + 1e-6)
            a_ref[s, :] = (x * r).astype(bf16)
    for b in range(blocks):
        z_ref[block(b), :] = jnp.dot(a_ref[block(b), :], one_ref[...], preferred_element_type=f32)
    for b in range(blocks):
        gram[block(b), :] = turned_dot(a_ref[block(b), :], a_ref[...]).astype(bf16)
        for s in chunks(b):
            z = z_ref[s, :] * c
            z_ref[s, :] = z
            hidden(s, z, xb, hn_ref, h_ref, sp_ref, r_ref)


def train_kernel(k_ref, got_ref, *refs):
    far, (ch1_out, ch2_out), near, refs = refs[:8], refs[8:10], refs[10:18], refs[18:]
    y_ref, ef_ref, g_ref, sum_ref, two_ref, w2_ref, hn1, eb_ref, u2_ref, ch1_ref, ch2_ref, sems, out_sems = refs
    depth = got_ref.shape[1]
    copies = []
    for x in range(4):
        for z in range(2):
            rows_of = two_ref.at[pl.ds((z * 4 + x) * depth, depth), :]
            copies.append(pltpu.make_async_copy(got_ref.at[x * 2 + z], rows_of, sems.at[x * 2 + z]))
    copies += [pltpu.make_async_copy(f, n, sems.at[8 + i]) for i, (f, n) in enumerate(zip(far, near))]
    for copy in copies:
        copy.start()
    hn0, xb, h_ref, sp, r_ref, gram, z_ref, a_ref = near
    total, width = xb.shape
    slots = total // 4
    rows = 3 * slots
    c = width**-0.5
    blocks = rows // BLOCK_ROWS
    k = k_ref[:1, :1]
    hn, w2 = hn0, two_ref
    for copy in copies[:9]:
        copy.wait()
    sent = []

    def send(kept, out, s):
        at = pl.ds(s.start, s.stop - s.start)
        copy = pltpu.make_async_copy(kept.at[at, :], out.at[at, :], out_sems.at[len(sent)])
        copy.start()
        sent.append(copy)

    def error(s):
        t = xb[s.start + slots : s.stop + slots, :].astype(f32)
        ef = (h_ref[s, :] + c * y_ref[s, :] - t) * k
        ef_ref[s, :] = ef
        eb_ref[s, :] = ef.astype(bf16)

    def back(s, step):
        q, h, r = y_ref[s, :], h_ref[s, :], r_ref[s, :1]
        qh = jnp.sum(q * h, axis=1, keepdims=True)
        m = (c / width) * r * r * r * qh
        g = sp[s, :] * (ef_ref[s, :] + (c * r) * q - m * h)
        if step == 0:
            sum_ref[s, :] = g
        elif step < STEPS - 1:
            sum_ref[s, :] = sum_ref[s, :] + g
        else:
            g = sum_ref[s, :] + g
        g_ref[s, :] = g.astype(bf16)

    for step in range(STEPS):
        last = step == STEPS - 1
        for b in range(blocks):
            if step > 0:
                for s in chunks(b):
                    z = z_ref[s, :] - y_ref[s, :]
                    if not last:
                        z_ref[s, :] = z
                    hidden(s, z, xb, hn1, h_ref, sp, r_ref)
                hn = hn1
            y_ref[block(b), :] = jnp.dot(hn[block(b), :], w2[...], preferred_element_type=f32)
        if step == 0:
            for copy in copies[9:]:
                copy.wait()
        for b in range(blocks):
            for s in chunks(b):
                error(s)
            y_ref[block(b), :] = turned_dot(eb_ref[block(b), :], w2[...])
        for q in range(width // 128):
            s = slice(q * 128, (q + 1) * 128)
            u2 = first_turned(hn[:, s], eb_ref[...])
            if step > 0:
                u2 = u2_ref[s, :] + u2
            if last:
                ch2_ref[s, :] = u2.astype(bf16)
                send(ch2_ref, ch2_out, s)
            else:
                u2_ref[s, :] = u2
                w2_ref[s, :] = (two_ref[s, :].astype(f32) - u2).astype(bf16)
        w2 = w2_ref
        for b in range(blocks):
            for s in chunks(b):
                back(s, step)
        if not last:
            for b in range(blocks):
                y_ref[block(b), :] = jnp.dot(gram[block(b), :], g_ref[...], preferred_element_type=f32)
    for q in range(width // 128):
        s = slice(q * 128, (q + 1) * 128)
        ch1_ref[s, :] = (first_turned(a_ref[:, s], g_ref[...]) * (1.0 / c)).astype(bf16)
        send(ch1_ref, ch1_out, s)
    for copy in sent:
        copy.wait()


def first_turned(a, b):
    return lax.dot_general(a, b, (((0,), (0,)), ((), ())), preferred_element_type=f32)


def prepare(recv, one):
    total, width = recv.shape
    rows = total // 4 * 3
    wide, thin = ((rows, width), f32), ((rows, width), bf16)
    made = [((total, width), bf16), thin, ((rows, rows), bf16), ((8, 128), f32), wide, thin, wide, wide, ((rows, 128), f32)]
    spec = pl.BlockSpec(memory_space=pltpu.VMEM)
    return pl.pallas_call(
        prepare_kernel,
        out_shape=[jax.ShapeDtypeStruct(*m) for m in made],
        in_specs=[spec] * 2,
        out_specs=[spec] * len(made),
        compiler_params=pltpu.CompilerParams(vmem_limit_bytes=PREP_VMEM),
        cost_estimate=cost(3 * 2 * rows * width * width, 20 * rows * width),
        name="prepare",
    )(recv, one)


def train(prepared, got):
    xb, a, gram, k, z, hn, h, sp, r = prepared
    rows, width = a.shape
    wide, thin, square = ((rows, width), f32), ((rows, width), bf16), ((width, width), bf16)
    kept = [wide, wide, thin, wide, square, square, thin, thin, ((width, width), f32), square, square]
    far = (hn, xb, h, sp, r, gram, z, a)
    hbm = pl.BlockSpec(memory_space=pltpu.HBM)
    return pl.pallas_call(
        train_kernel,
        out_shape=[jax.ShapeDtypeStruct(*square)] * 2,
        in_specs=[pl.BlockSpec(memory_space=pltpu.VMEM)] + [hbm] * (1 + len(far)),
        out_specs=[hbm] * 2,
        scratch_shapes=[pltpu.VMEM(f.shape, f.dtype) for f in far]
        + [pltpu.VMEM(*m) for m in kept]
        + [pltpu.SemaphoreType.DMA((8 + len(far),)), pltpu.SemaphoreType.DMA((2 * (width // 128),))],
        compiler_params=pltpu.CompilerParams(vmem_limit_bytes=TRAIN_VMEM),
        cost_estimate=cost(12 * 2 * rows * width * width, 20 * rows * width),
        name="train",
    )(k, got, *far)


def a2a(array, axis):
    return lax.all_to_all(array, axis, 0, 0, tiled=True)


def swap(array, bit):
    n = lax.axis_size("col")
    return lax.ppermute(array, "col", [(i, i ^ bit) for i in range(n)])


Z_BIT, Y_BITS, CORE_BIT = 8, (2, 4, 6), 1


def assemble_kernel(places_ref, near_ref, far_ref, out_ref):
    n = near_ref.shape[0]
    for k in range(n):
        out_ref[places_ref[k]] = near_ref[k]
        out_ref[places_ref[n + k]] = far_ref[k]


def pair_two(own, other):
    z = lax.axis_index("row") >> 2
    pair = jnp.stack([jnp.where(z == 0, own, other), jnp.where(z == 0, other, own)])
    return jnp.broadcast_to(pair, (4, *pair.shape))


def gather_two(sent):
    groups = [[0, 1, 2, 3], [4, 5, 6, 7]]
    got = lax.all_to_all(sent, "row", 0, 0, tiled=True, axis_index_groups=groups)
    return got.reshape(8, *got.shape[2:])


def gather_near(own, other):
    pair = jnp.stack([own, other])
    return jnp.concatenate([pair, *(swap(pair, bit) for bit in Y_BITS)])


def gather_far(near):
    me = lax.axis_index("col")
    far = swap(near, CORE_BIT)
    order = jnp.array([y | z for y in (0, *Y_BITS) for z in (0, Z_BIT)], jnp.int32)
    places = jnp.concatenate([me ^ order, me ^ order ^ CORE_BIT])
    n = 2 * near.shape[0]
    return pl.pallas_call(
        assemble_kernel,
        out_shape=jax.ShapeDtypeStruct((n, *near.shape[1:]), near.dtype),
        in_specs=[pl.BlockSpec(memory_space=pltpu.SMEM)] + [pl.BlockSpec(memory_space=pltpu.VMEM)] * 2,
        out_specs=pl.BlockSpec(memory_space=pltpu.VMEM),
        compiler_params=pltpu.CompilerParams(vmem_limit_bytes=8 << 20),
        cost_estimate=cost(0, 2 * n * near.shape[1] * near.shape[2] * 2),
        name="assemble",
    )(places, near, far)


def pick(array, at, axis):
    return lax.dynamic_index_in_dim(array, at, axis, keepdims=False)


def reduce_one(change):
    me = lax.axis_index("col")
    me = me.astype(jnp.uint32)
    z, y, core = me >> 3, (me >> 1) & 3, me & 1
    width = change.shape[1]
    tiles = change.reshape(2, 4, 2, -1, width)
    got = swap(pick(tiles, core ^ 1, 2), CORE_BIT)
    part = (pick(tiles, core, 2).astype(f32) + got.astype(f32)).astype(bf16)
    got = [swap(pick(part, y ^ jnp.uint32(bit // 2), 1), bit) for bit in Y_BITS]
    part = pick(part, y, 1).astype(f32)
    for g in got:
        part = part + g.astype(f32)
    part = part.astype(bf16)
    got = swap(pick(part, z ^ 1, 0), Z_BIT)
    return pick(part, z, 0).astype(f32) + got.astype(f32)


def shards(docs, routes, level_one, level_two, moment_one, moment_two):
    n_row = lax.axis_size("row")
    n_col = lax.axis_size("col")
    count, length, width = docs.shape
    own_one = level_one[0].astype(bf16)
    own_two = level_two[0].astype(bf16)
    other_one = swap(own_one, Z_BIT)
    other_two = lax.ppermute(own_two, "row", [(i, i ^ 4) for i in range(n_row)])
    outgoing = dispatch(routes, docs)
    other_one, other_two, outgoing = lax.optimization_barrier((other_one, other_two, outgoing))
    recv = a2a(outgoing.reshape(n_row * n_col, length * CAPACITY, width), ("row", "col"))
    whole_one = gather_far(gather_near(own_one, other_one)).reshape(width, width)
    recv, sent = lax.optimization_barrier((recv, pair_two(own_two, other_two)))
    got = gather_two(sent)
    change_one, change_two = train(prepare(recv.reshape(-1, width), whole_one), got)
    got_two = a2a(change_two.reshape(n_row, -1, width), "row")
    delta_one = (reduce_one(change_one) / n_col)[None]
    delta_two = (jnp.sum(got_two.astype(f32), axis=0) / n_row)[None]
    next_moment_one = momentum_decay * moment_one + delta_one
    next_moment_two = momentum_decay * moment_two + delta_two
    new_one = level_one - outer_rate * (delta_one + momentum_decay * next_moment_one)
    new_two = level_two - outer_rate * (delta_two + momentum_decay * next_moment_two)
    return (new_one, new_two, next_moment_one, next_moment_two)


def solution(mesh):
    placed = (
        P(("row", "col"), None, None),
        P(("row", "col"), None),
        P("row", "col", None),
        P("col", "row", None),
        P("row", "col", None),
        P("col", "row", None),
    )
    return jax.shard_map(
        shards,
        mesh=mesh,
        in_specs=placed,
        out_specs=(
            P("row", "col", None),
            P("col", "row", None),
            P("row", "col", None),
            P("col", "row", None),
        ),
        check_vma=False,
    )
```

```python
import functools

import jax
import jax.numpy as jnp
from jax import lax
from jax.experimental import pallas as pl
from jax.experimental.pallas import tpu as pltpu
from jax.sharding import PartitionSpec as P

STEPS = 3
inner_rate = 64.0
outer_rate = 0.7
momentum_decay = 0.9
EMPTY = 16.0
CAPACITY = 2

f32, bf16 = jnp.float32, jnp.bfloat16


def dispatch_kernel(length, routes_ref, docs_ref, out_ref):
    count = routes_ref.shape[1]
    rows = out_ref.shape[0]
    per = length * CAPACITY
    route = jnp.broadcast_to(routes_ref[...].astype(f32), (count, count))
    turned = route.T
    i = lax.broadcasted_iota(jnp.int32, (count, count), 0)
    j = lax.broadcasted_iota(jnp.int32, (count, count), 1)
    earlier = jnp.where((route == turned) & (i < j), 1.0, 0.0)
    rank = jnp.sum(earlier, axis=0, keepdims=True)
    key = (routes_ref[...].astype(f32) * per + rank).astype(jnp.int32)
    keys = jnp.concatenate([key + CAPACITY * t for t in range(length)], axis=1)
    step = 256
    for b in range(rows // step):
        at = lax.broadcasted_iota(jnp.int32, (step, length * count), 0) + b * step
        hot = jnp.where(at == keys, 1.0, 0.0)
        filled = jnp.sum(hot, axis=1, keepdims=True)
        moved = jnp.dot(hot.astype(bf16), docs_ref[...], preferred_element_type=f32)
        out_ref[b * step : (b + 1) * step, :] = (moved + EMPTY * (1.0 - filled)).astype(bf16)


def cost(flops, moved):
    return pl.CostEstimate(flops=flops, transcendentals=0, bytes_accessed=moved)


def dispatch(routes, docs):
    count, length, width = docs.shape
    paths = count
    planes = jnp.transpose(docs, (1, 0, 2)).reshape(length * count, width)
    rows = 128 * length * CAPACITY
    return pl.pallas_call(
        functools.partial(dispatch_kernel, length),
        out_shape=jax.ShapeDtypeStruct((rows, width), bf16),
        in_specs=[pl.BlockSpec(memory_space=pltpu.VMEM)] * 2,
        out_specs=pl.BlockSpec(memory_space=pltpu.VMEM),
        compiler_params=pltpu.CompilerParams(vmem_limit_bytes=24 << 20),
        cost_estimate=cost(2 * rows * length * count * width, 4 * rows * width),
        name="dispatch",
    )(routes.reshape(1, count), planes)


BLOCK_ROWS = 256
CHUNK = 32
TRAIN_VMEM = 31 << 20
TAIL_VMEM = 4 << 20


def train_kernel(
    recv_ref, one_far, two_far,
    ch1_ref, hn_ref, eb_ref, u2_ref,
    xb, a_ref, gram, z_ref, h_ref, sp_ref, r_ref, y_ref, ef_ref, g_ref, sum_ref, w2_ref, one_ref, two_ref, sems,
):
    one_copy = pltpu.make_async_copy(one_far, one_ref, sems.at[0])
    two_copy = pltpu.make_async_copy(two_far, two_ref, sems.at[1])
    one_copy.start()
    two_copy.start()
    width = recv_ref.shape[1]
    total = recv_ref.shape[0]
    slots = total // 4
    rows = 3 * slots
    c = width**-0.5
    blocks = rows // BLOCK_ROWS
    i = lax.broadcasted_iota(jnp.int32, (128, 128), 0)
    j = lax.broadcasted_iota(jnp.int32, (128, 128), 1)
    source = ((i % 32) // 2) * 8 + (i // 32) * 2 + i % 2
    perm = jnp.where(j == source, 1.0, 0.0).astype(bf16)
    empties = jnp.zeros((1, 128), f32)
    for b in range(total // 128):
        v = recv_ref[b * 128 : (b + 1) * 128, :].astype(f32)
        gone = v > 7.0
        empties = empties + jnp.sum(jnp.where(gone[:, :128], 1.0, 0.0), axis=0, keepdims=True)
        v = jnp.where(gone, 0.0, v).astype(bf16)
        p = jnp.dot(perm, v, preferred_element_type=f32).astype(bf16)
        for t in range(4):
            xb[t * slots + b * 32 : t * slots + (b + 1) * 32, :] = p[t * 32 : (t + 1) * 32, :]
    valid = slots - jnp.max(empties, axis=1, keepdims=True) * 0.25
    inv = 1.0 / (3.0 * valid)
    k = inner_rate * c * inv

    def chunks(b, size=CHUNK):
        for q in range(BLOCK_ROWS // size):
            at = b * BLOCK_ROWS + q * size
            yield slice(at, at + size)

    for b in range(blocks):
        for s in chunks(b):
            x = xb[s, :].astype(f32)
            r = lax.rsqrt(jnp.sum(x * x, axis=1, keepdims=True) * (1.0 / width) + 1e-6)
            a_ref[s, :] = (x * r).astype(bf16)

    def block(b):
        return slice(b * BLOCK_ROWS, (b + 1) * BLOCK_ROWS)

    one_copy.wait()
    for b in range(blocks):
        z_ref[block(b), :] = jnp.dot(a_ref[block(b), :], one_ref[...], preferred_element_type=f32)
    for b in range(blocks):
        gram[block(b), :] = lax.dot_general(
            a_ref[block(b), :], a_ref[...], (((1,), (1,)), ((), ())), preferred_element_type=f32
        ).astype(bf16)

    def hidden(s, step):
        if step == 0:
            z = z_ref[s, :] * c
        else:
            z = z_ref[s, :] - y_ref[s, :]
        if step < STEPS - 1:
            z_ref[s, :] = z
        sg = 0.5 * jnp.tanh(0.5 * z) + 0.5
        si = z * sg
        h = xb[s, :].astype(f32) + si
        sp_ref[s, :] = (sg + si * (1.0 - sg)) * c
        r = lax.rsqrt(jnp.sum(h * h, axis=1, keepdims=True) * (1.0 / width) + 1e-6)
        h_ref[s, :] = h
        r_ref[s, :] = jnp.broadcast_to(r, (h.shape[0], 128))
        hn_ref[s, :] = (h * r).astype(bf16)

    def error(s):
        t = xb[s.start + slots : s.stop + slots, :].astype(f32)
        ef = (h_ref[s, :] + c * y_ref[s, :] - t) * k
        ef_ref[s, :] = ef
        eb_ref[s, :] = ef.astype(bf16)

    def back(s, step):
        q, h, r = y_ref[s, :], h_ref[s, :], r_ref[s, :1]
        qh = jnp.sum(q * h, axis=1, keepdims=True)
        m = (c / width) * r * r * r * qh
        g = sp_ref[s, :] * (ef_ref[s, :] + (c * r) * q - m * h)
        if step == 0:
            sum_ref[s, :] = g
        elif step < STEPS - 1:
            sum_ref[s, :] = sum_ref[s, :] + g
        else:
            g = sum_ref[s, :] + g
        g_ref[s, :] = g.astype(bf16)

    two_copy.wait()
    w2 = two_ref
    for step in range(STEPS):
        last = step == STEPS - 1
        for b in range(blocks):
            for s in chunks(b):
                hidden(s, step)
            y_ref[block(b), :] = jnp.dot(hn_ref[block(b), :], w2[...], preferred_element_type=f32)
        for b in range(blocks):
            for s in chunks(b):
                error(s)
            y_ref[block(b), :] = lax.dot_general(
                eb_ref[block(b), :], w2[...], (((1,), (1,)), ((), ())), preferred_element_type=f32
            )
        if not last:
            for q in range(width // 128):
                s = slice(q * 128, (q + 1) * 128)
                u2 = first_turned(hn_ref[:, s], eb_ref[...])
                if step > 0:
                    u2 = u2_ref[s, :] + u2
                u2_ref[s, :] = u2
                w2_ref[s, :] = (two_ref[s, :].astype(f32) - u2).astype(bf16)
            w2 = w2_ref
        for b in range(blocks):
            for s in chunks(b):
                back(s, step)
        if not last:
            for b in range(blocks):
                y_ref[block(b), :] = jnp.dot(gram[block(b), :], g_ref[...], preferred_element_type=f32)
    for q in range(width // 128):
        s = slice(q * 128, (q + 1) * 128)
        ch1_ref[s, :] = (first_turned(a_ref[:, s], g_ref[...]) * (1.0 / c)).astype(bf16)


def first_turned(a, b):
    return lax.dot_general(a, b, (((0,), (0,)), ((), ())), preferred_element_type=f32)


def tail_kernel(hn_ref, eb_ref, u2_ref, ch2_ref):
    width = hn_ref.shape[1]
    for q in range(width // 128):
        s = slice(q * 128, (q + 1) * 128)
        ch2_ref[s, :] = (u2_ref[s, :] + first_turned(hn_ref[:, s], eb_ref[...])).astype(bf16)


def train(recv, one, two):
    total, width = recv.shape
    rows = total // 4 * 3
    wide, thin, square = ((rows, width), f32), ((rows, width), bf16), (width, width)
    made = [(square, bf16), thin, thin, (square, f32)]
    kept = [
        ((total, width), bf16), thin, ((rows, rows), bf16), wide, wide, wide,
        ((rows, 128), f32), wide, wide, thin, wide, (square, bf16), (square, bf16), (square, bf16),
    ]
    spec = pl.BlockSpec(memory_space=pltpu.VMEM)
    change_one, *rest = pl.pallas_call(
        train_kernel,
        out_shape=[jax.ShapeDtypeStruct(*m) for m in made],
        in_specs=[spec] + [pl.BlockSpec(memory_space=pltpu.HBM)] * 2,
        out_specs=[spec] * 4,
        scratch_shapes=[pltpu.VMEM(*m) for m in kept] + [pltpu.SemaphoreType.DMA((2,))],
        compiler_params=pltpu.CompilerParams(vmem_limit_bytes=TRAIN_VMEM),
        cost_estimate=cost(14 * 2 * rows * width * width, 30 * rows * width),
        name="train",
    )(recv, one, two)
    change_two = pl.pallas_call(
        tail_kernel,
        out_shape=jax.ShapeDtypeStruct(square, bf16),
        in_specs=[spec] * 3,
        out_specs=spec,
        compiler_params=pltpu.CompilerParams(vmem_limit_bytes=TAIL_VMEM),
        cost_estimate=cost(2 * rows * width * width, 10 * rows * width),
        name="tail",
    )(*rest)
    return change_one, change_two


def a2a(array, axis):
    return lax.all_to_all(array, axis, 0, 0, tiled=True)


def swap(array, bit):
    n = lax.axis_size("col")
    return lax.ppermute(array, "col", [(i, i ^ bit) for i in range(n)])


Z_BIT, Y_BITS, CORE_BIT = 8, (2, 4, 6), 1


def assemble_kernel(places_ref, near_ref, far_ref, out_ref):
    n = near_ref.shape[0]
    for k in range(n):
        out_ref[places_ref[k]] = near_ref[k]
        out_ref[places_ref[n + k]] = far_ref[k]


def gather_near(own, other):
    pair = jnp.stack([own, other])
    return jnp.concatenate([pair, *(swap(pair, bit) for bit in Y_BITS)])


def gather_far(near):
    me = lax.axis_index("col")
    far = swap(near, CORE_BIT)
    order = jnp.array([y | z for y in (0, *Y_BITS) for z in (0, Z_BIT)], jnp.int32)
    places = jnp.concatenate([me ^ order, me ^ order ^ CORE_BIT])
    n = 2 * near.shape[0]
    return pl.pallas_call(
        assemble_kernel,
        out_shape=jax.ShapeDtypeStruct((n, *near.shape[1:]), near.dtype),
        in_specs=[pl.BlockSpec(memory_space=pltpu.SMEM)] + [pl.BlockSpec(memory_space=pltpu.VMEM)] * 2,
        out_specs=pl.BlockSpec(memory_space=pltpu.VMEM),
        compiler_params=pltpu.CompilerParams(vmem_limit_bytes=8 << 20),
        cost_estimate=cost(0, 2 * n * near.shape[1] * near.shape[2] * 2),
        name="assemble",
    )(places, near, far)


def pick(array, at, axis):
    return lax.dynamic_index_in_dim(array, at, axis, keepdims=False)


def reduce_one(change):
    me = lax.axis_index("col")
    me = me.astype(jnp.uint32)
    z, y, core = me >> 3, (me >> 1) & 3, me & 1
    width = change.shape[1]
    tiles = change.reshape(2, 4, 2, -1, width)
    got = swap(pick(tiles, core ^ 1, 2), CORE_BIT)
    part = (pick(tiles, core, 2).astype(f32) + got.astype(f32)).astype(bf16)
    got = [swap(pick(part, y ^ jnp.uint32(bit // 2), 1), bit) for bit in Y_BITS]
    part = pick(part, y, 1).astype(f32)
    for g in got:
        part = part + g.astype(f32)
    part = part.astype(bf16)
    got = swap(pick(part, z ^ 1, 0), Z_BIT)
    return pick(part, z, 0), got


def shards(docs, routes, level_one, level_two, moment_one, moment_two):
    n_row = lax.axis_size("row")
    n_col = lax.axis_size("col")
    count, length, width = docs.shape
    own_one = level_one[0].astype(bf16)
    other_one = swap(own_one, Z_BIT)
    own_two = level_two.astype(bf16)
    sent_two = jnp.broadcast_to(own_two, (n_row, *own_two.shape[1:]))
    other_one, sent_two = lax.optimization_barrier((other_one, sent_two))
    whole_two = a2a(sent_two, "row").reshape(width, width)
    outgoing = dispatch(routes, docs)
    near = gather_near(own_one, other_one)
    near, outgoing = lax.optimization_barrier((near, outgoing))
    whole_one = gather_far(near).reshape(width, width)
    recv = a2a(outgoing.reshape(n_row * n_col, length * CAPACITY, width), ("row", "col"))
    change_one, change_two = train(recv.reshape(-1, width), whole_one, whole_two)
    part, got_one = reduce_one(change_one)
    got_two = a2a(change_two.reshape(n_row, -1, width), "row")
    delta_two = (jnp.sum(got_two.astype(f32), axis=0) / n_row)[None]
    next_moment_two = momentum_decay * moment_two + delta_two
    new_two = level_two - outer_rate * (delta_two + momentum_decay * next_moment_two)
    got_one, new_two, next_moment_two = lax.optimization_barrier((got_one, new_two, next_moment_two))
    delta_one = ((part.astype(f32) + got_one.astype(f32)) / n_col)[None]
    next_moment_one = momentum_decay * moment_one + delta_one
    new_one = level_one - outer_rate * (delta_one + momentum_decay * next_moment_one)
    return (new_one, new_two, next_moment_one, next_moment_two)


def solution(mesh):
    placed = (
        P(("row", "col"), None, None),
        P(("row", "col"), None),
        P("row", "col", None),
        P("col", "row", None),
        P("row", "col", None),
        P("col", "row", None),
    )
    return jax.shard_map(
        shards,
        mesh=mesh,
        in_specs=placed,
        out_specs=(
            P("row", "col", None),
            P("col", "row", None),
            P("row", "col", None),
            P("col", "row", None),
        ),
        check_vma=False,
    )
```

```python
import functools

import jax
import jax.numpy as jnp
from jax import lax
from jax.experimental import pallas as pl
from jax.experimental.pallas import tpu as pltpu
from jax.sharding import PartitionSpec as P

STEPS = 3
inner_rate = 64.0
outer_rate = 0.7
momentum_decay = 0.9
EMPTY = 16.0
CAPACITY = 2

f32, bf16 = jnp.float32, jnp.bfloat16


def dispatch_kernel(length, routes_ref, docs_ref, out_ref):
    count = routes_ref.shape[1]
    rows = out_ref.shape[0]
    per = length * CAPACITY
    route = jnp.broadcast_to(routes_ref[...].astype(f32), (count, count))
    turned = route.T
    i = lax.broadcasted_iota(jnp.int32, (count, count), 0)
    j = lax.broadcasted_iota(jnp.int32, (count, count), 1)
    earlier = jnp.where((route == turned) & (i < j), 1.0, 0.0)
    rank = jnp.sum(earlier, axis=0, keepdims=True)
    key = (routes_ref[...].astype(f32) * per + rank).astype(jnp.int32)
    keys = jnp.concatenate([key + CAPACITY * t for t in range(length)], axis=1)
    step = 256
    for b in range(rows // step):
        at = lax.broadcasted_iota(jnp.int32, (step, length * count), 0) + b * step
        hot = jnp.where(at == keys, 1.0, 0.0)
        filled = jnp.sum(hot, axis=1, keepdims=True)
        moved = jnp.dot(hot.astype(bf16), docs_ref[...], preferred_element_type=f32)
        out_ref[b * step : (b + 1) * step, :] = (moved + EMPTY * (1.0 - filled)).astype(bf16)


def cost(flops, moved):
    return pl.CostEstimate(flops=flops, transcendentals=0, bytes_accessed=moved)


def dispatch(routes, docs):
    count, length, width = docs.shape
    paths = count
    planes = jnp.transpose(docs, (1, 0, 2)).reshape(length * count, width)
    rows = 128 * length * CAPACITY
    return pl.pallas_call(
        functools.partial(dispatch_kernel, length),
        out_shape=jax.ShapeDtypeStruct((rows, width), bf16),
        in_specs=[pl.BlockSpec(memory_space=pltpu.VMEM)] * 2,
        out_specs=pl.BlockSpec(memory_space=pltpu.VMEM),
        compiler_params=pltpu.CompilerParams(vmem_limit_bytes=24 << 20),
        cost_estimate=cost(2 * rows * length * count * width, 4 * rows * width),
        name="dispatch",
    )(routes.reshape(1, count), planes)


BLOCK_ROWS = 256
CHUNK = 32
TRAIN_VMEM = 38 << 20


def train_kernel(
    recv_ref, one_far, two_far,
    ch1_ref, ch2_out,
    ch2_ref, hn_ref, eb_ref, u2_ref, xb, a_ref, gram, z_ref, h_ref, sp_ref, r_ref, y_ref, ef_ref, g_ref, sum_ref, w2_ref, one_ref, two_ref, sems,
):
    one_copy = pltpu.make_async_copy(one_far, one_ref, sems.at[0])
    two_copy = pltpu.make_async_copy(two_far, two_ref, sems.at[1])
    one_copy.start()
    two_copy.start()
    width = recv_ref.shape[1]
    total = recv_ref.shape[0]
    slots = total // 4
    rows = 3 * slots
    c = width**-0.5
    blocks = rows // BLOCK_ROWS
    i = lax.broadcasted_iota(jnp.int32, (128, 128), 0)
    j = lax.broadcasted_iota(jnp.int32, (128, 128), 1)
    source = ((i % 32) // 2) * 8 + (i // 32) * 2 + i % 2
    perm = jnp.where(j == source, 1.0, 0.0).astype(bf16)
    empties = jnp.zeros((1, 128), f32)
    for b in range(total // 128):
        v = recv_ref[b * 128 : (b + 1) * 128, :].astype(f32)
        gone = v > 7.0
        empties = empties + jnp.sum(jnp.where(gone[:, :128], 1.0, 0.0), axis=0, keepdims=True)
        v = jnp.where(gone, 0.0, v).astype(bf16)
        p = jnp.dot(perm, v, preferred_element_type=f32).astype(bf16)
        for t in range(4):
            xb[t * slots + b * 32 : t * slots + (b + 1) * 32, :] = p[t * 32 : (t + 1) * 32, :]
    valid = slots - jnp.max(empties, axis=1, keepdims=True) * 0.25
    inv = 1.0 / (3.0 * valid)
    k = inner_rate * c * inv

    def chunks(b, size=CHUNK):
        for q in range(BLOCK_ROWS // size):
            at = b * BLOCK_ROWS + q * size
            yield slice(at, at + size)

    for b in range(blocks):
        for s in chunks(b):
            x = xb[s, :].astype(f32)
            r = lax.rsqrt(jnp.sum(x * x, axis=1, keepdims=True) * (1.0 / width) + 1e-6)
            a_ref[s, :] = (x * r).astype(bf16)

    def block(b):
        return slice(b * BLOCK_ROWS, (b + 1) * BLOCK_ROWS)

    one_copy.wait()
    for b in range(blocks):
        z_ref[block(b), :] = jnp.dot(a_ref[block(b), :], one_ref[...], preferred_element_type=f32)
    for b in range(blocks):
        gram[block(b), :] = lax.dot_general(
            a_ref[block(b), :], a_ref[...], (((1,), (1,)), ((), ())), preferred_element_type=f32
        ).astype(bf16)

    def hidden(s, step):
        if step == 0:
            z = z_ref[s, :] * c
        else:
            z = z_ref[s, :] - y_ref[s, :]
        if step < STEPS - 1:
            z_ref[s, :] = z
        sg = 0.5 * jnp.tanh(0.5 * z) + 0.5
        si = z * sg
        h = xb[s, :].astype(f32) + si
        sp_ref[s, :] = (sg + si * (1.0 - sg)) * c
        r = lax.rsqrt(jnp.sum(h * h, axis=1, keepdims=True) * (1.0 / width) + 1e-6)
        h_ref[s, :] = h
        r_ref[s, :] = jnp.broadcast_to(r, (h.shape[0], 128))
        hn_ref[s, :] = (h * r).astype(bf16)

    def error(s):
        t = xb[s.start + slots : s.stop + slots, :].astype(f32)
        ef = (h_ref[s, :] + c * y_ref[s, :] - t) * k
        ef_ref[s, :] = ef
        eb_ref[s, :] = ef.astype(bf16)

    def back(s, step):
        q, h, r = y_ref[s, :], h_ref[s, :], r_ref[s, :1]
        qh = jnp.sum(q * h, axis=1, keepdims=True)
        m = (c / width) * r * r * r * qh
        g = sp_ref[s, :] * (ef_ref[s, :] + (c * r) * q - m * h)
        if step == 0:
            sum_ref[s, :] = g
        elif step < STEPS - 1:
            sum_ref[s, :] = sum_ref[s, :] + g
        else:
            g = sum_ref[s, :] + g
        g_ref[s, :] = g.astype(bf16)

    two_copy.wait()
    w2 = two_ref
    sent = []
    columns = [slice(q * 128, (q + 1) * 128) for q in range(width // 128)]

    def pulled(b):
        y_ref[block(b), :] = jnp.dot(gram[block(b), :], g_ref[...], preferred_element_type=f32)

    def forward(b, step):
        for s in chunks(b):
            hidden(s, step)
        y_ref[block(b), :] = jnp.dot(hn_ref[block(b), :], w2[...], preferred_element_type=f32)

    def turn(b):
        for s in chunks(b):
            error(s)
        y_ref[block(b), :] = lax.dot_general(
            eb_ref[block(b), :], w2[...], (((1,), (1,)), ((), ())), preferred_element_type=f32
        )

    def change(s, step):
        u2 = first_turned(hn_ref[:, s], eb_ref[...])
        if step > 0:
            u2 = u2_ref[s, :] + u2
        if step == STEPS - 1:
            ch2_ref[s, :] = u2.astype(bf16)
            copy = pltpu.make_async_copy(ch2_ref.at[s, :], ch2_out.at[s, :], sems.at[2 + len(sent)])
            copy.start()
            sent.append(copy)
        else:
            u2_ref[s, :] = u2
            w2_ref[s, :] = (two_ref[s, :].astype(f32) - u2).astype(bf16)

    for step in range(STEPS):
        for b in range(blocks + 2):
            if step > 0 and b < blocks:
                pulled(b)
            if 1 <= b <= blocks:
                forward(b - 1, step)
            if b >= 2:
                turn(b - 2)
        pending = [s for b in range(blocks) for s in chunks(b)]
        share = -(-len(pending) // len(columns))
        for q, s in enumerate(columns):
            change(s, step)
            for p in pending[q * share : (q + 1) * share]:
                back(p, step)
        w2 = w2_ref
    for s in columns:
        ch1_ref[s, :] = (first_turned(a_ref[:, s], g_ref[...]) * (1.0 / c)).astype(bf16)
    for copy in sent:
        copy.wait()


def first_turned(a, b):
    return lax.dot_general(a, b, (((0,), (0,)), ((), ())), preferred_element_type=f32)


def train(recv, one, two):
    total, width = recv.shape
    rows = total // 4 * 3
    wide, thin, square = ((rows, width), f32), ((rows, width), bf16), (width, width)
    kept = [
        (square, bf16), thin, thin, (square, f32),
        ((total, width), bf16), thin, ((rows, rows), bf16), wide, wide, wide,
        ((rows, 128), f32), wide, wide, thin, wide, (square, bf16), (square, bf16), (square, bf16),
    ]
    spec = pl.BlockSpec(memory_space=pltpu.VMEM)
    return pl.pallas_call(
        train_kernel,
        out_shape=[jax.ShapeDtypeStruct(square, bf16)] * 2,
        in_specs=[spec] + [pl.BlockSpec(memory_space=pltpu.HBM)] * 2,
        out_specs=[spec, pl.BlockSpec(memory_space=pltpu.HBM)],
        scratch_shapes=[pltpu.VMEM(*m) for m in kept] + [pltpu.SemaphoreType.DMA((2 + width // 128,))],
        compiler_params=pltpu.CompilerParams(vmem_limit_bytes=TRAIN_VMEM),
        cost_estimate=cost(14 * 2 * rows * width * width, 30 * rows * width),
        name="train",
    )(recv, one, two)


def a2a(array, axis):
    return lax.all_to_all(array, axis, 0, 0, tiled=True)


def swap(array, bit):
    n = lax.axis_size("col")
    return lax.ppermute(array, "col", [(i, i ^ bit) for i in range(n)])


Z_BIT, Y_BITS, CORE_BIT = 8, (2, 4, 6), 1


def assemble_kernel(places_ref, near_ref, far_ref, out_ref):
    n = near_ref.shape[0]
    for k in range(n):
        out_ref[places_ref[k]] = near_ref[k]
        out_ref[places_ref[n + k]] = far_ref[k]


def gather_near(own, other):
    pair = jnp.stack([own, other])
    return jnp.concatenate([pair, *(swap(pair, bit) for bit in Y_BITS)])


def gather_far(near):
    me = lax.axis_index("col")
    far = swap(near, CORE_BIT)
    order = jnp.array([y | z for y in (0, *Y_BITS) for z in (0, Z_BIT)], jnp.int32)
    places = jnp.concatenate([me ^ order, me ^ order ^ CORE_BIT])
    n = 2 * near.shape[0]
    return pl.pallas_call(
        assemble_kernel,
        out_shape=jax.ShapeDtypeStruct((n, *near.shape[1:]), near.dtype),
        in_specs=[pl.BlockSpec(memory_space=pltpu.SMEM)] + [pl.BlockSpec(memory_space=pltpu.VMEM)] * 2,
        out_specs=pl.BlockSpec(memory_space=pltpu.VMEM),
        compiler_params=pltpu.CompilerParams(vmem_limit_bytes=8 << 20),
        cost_estimate=cost(0, 2 * n * near.shape[1] * near.shape[2] * 2),
        name="assemble",
    )(places, near, far)


def pick(array, at, axis):
    return lax.dynamic_index_in_dim(array, at, axis, keepdims=False)


def reduce_one(change):
    me = lax.axis_index("col")
    me = me.astype(jnp.uint32)
    z, y, core = me >> 3, (me >> 1) & 3, me & 1
    width = change.shape[1]
    tiles = change.reshape(2, 4, 2, -1, width)
    got = swap(pick(tiles, core ^ 1, 2), CORE_BIT)
    part = (pick(tiles, core, 2).astype(f32) + got.astype(f32)).astype(bf16)
    got = [swap(pick(part, y ^ jnp.uint32(bit // 2), 1), bit) for bit in Y_BITS]
    part = pick(part, y, 1).astype(f32)
    for g in got:
        part = part + g.astype(f32)
    part = part.astype(bf16)
    got = swap(pick(part, z ^ 1, 0), Z_BIT)
    return pick(part, z, 0), got


def shards(docs, routes, level_one, level_two, moment_one, moment_two):
    n_row = lax.axis_size("row")
    n_col = lax.axis_size("col")
    count, length, width = docs.shape
    own_one = level_one[0].astype(bf16)
    other_one = swap(own_one, Z_BIT)
    own_two = level_two.astype(bf16)
    sent_two = jnp.broadcast_to(own_two, (n_row, *own_two.shape[1:]))
    other_one, sent_two = lax.optimization_barrier((other_one, sent_two))
    whole_two = a2a(sent_two, "row").reshape(width, width)
    outgoing = dispatch(routes, docs)
    near = gather_near(own_one, other_one)
    near, outgoing = lax.optimization_barrier((near, outgoing))
    whole_one = gather_far(near).reshape(width, width)
    recv = a2a(outgoing.reshape(n_row * n_col, length * CAPACITY, width), ("row", "col"))
    change_one, change_two = train(recv.reshape(-1, width), whole_one, whole_two)
    part, got_one = reduce_one(change_one)
    got_two = a2a(change_two.reshape(n_row, -1, width), "row")
    delta_two = (jnp.sum(got_two.astype(f32), axis=0) / n_row)[None]
    next_moment_two = momentum_decay * moment_two + delta_two
    new_two = level_two - outer_rate * (delta_two + momentum_decay * next_moment_two)
    got_one, new_two, next_moment_two = lax.optimization_barrier((got_one, new_two, next_moment_two))
    delta_one = ((part.astype(f32) + got_one.astype(f32)) / n_col)[None]
    next_moment_one = momentum_decay * moment_one + delta_one
    new_one = level_one - outer_rate * (delta_one + momentum_decay * next_moment_one)
    return (new_one, new_two, next_moment_one, next_moment_two)


def solution(mesh):
    placed = (
        P(("row", "col"), None, None),
        P(("row", "col"), None),
        P("row", "col", None),
        P("col", "row", None),
        P("row", "col", None),
        P("col", "row", None),
    )
    return jax.shard_map(
        shards,
        mesh=mesh,
        in_specs=placed,
        out_specs=(
            P("row", "col", None),
            P("col", "row", None),
            P("row", "col", None),
            P("col", "row", None),
        ),
        check_vma=False,
    )
```

```python
import functools

import jax
import jax.numpy as jnp
from jax import lax
from jax.experimental import pallas as pl
from jax.experimental.pallas import tpu as pltpu
from jax.sharding import PartitionSpec as P

STEPS = 3
inner_rate = 64.0
outer_rate = 0.7
momentum_decay = 0.9
EMPTY = 16.0
CAPACITY = 2

f32, bf16 = jnp.float32, jnp.bfloat16


def dispatch_kernel(length, routes_ref, docs_ref, out_ref):
    count = routes_ref.shape[1]
    rows = out_ref.shape[0]
    per = length * CAPACITY
    route = jnp.broadcast_to(routes_ref[...].astype(f32), (count, count))
    turned = route.T
    i = lax.broadcasted_iota(jnp.int32, (count, count), 0)
    j = lax.broadcasted_iota(jnp.int32, (count, count), 1)
    earlier = jnp.where((route == turned) & (i < j), 1.0, 0.0)
    rank = jnp.sum(earlier, axis=0, keepdims=True)
    key = (routes_ref[...].astype(f32) * per + rank).astype(jnp.int32)
    keys = jnp.concatenate([key + CAPACITY * t for t in range(length)], axis=1)
    step = 256
    for b in range(rows // step):
        at = lax.broadcasted_iota(jnp.int32, (step, length * count), 0) + b * step
        hot = jnp.where(at == keys, 1.0, 0.0)
        filled = jnp.sum(hot, axis=1, keepdims=True)
        moved = jnp.dot(hot.astype(bf16), docs_ref[...], preferred_element_type=f32)
        out_ref[b * step : (b + 1) * step, :] = (moved + EMPTY * (1.0 - filled)).astype(bf16)


def cost(flops, moved):
    return pl.CostEstimate(flops=flops, transcendentals=0, bytes_accessed=moved)


def dispatch(routes, docs):
    count, length, width = docs.shape
    paths = count
    planes = jnp.transpose(docs, (1, 0, 2)).reshape(length * count, width)
    rows = 128 * length * CAPACITY
    return pl.pallas_call(
        functools.partial(dispatch_kernel, length),
        out_shape=jax.ShapeDtypeStruct((rows, width), bf16),
        in_specs=[pl.BlockSpec(memory_space=pltpu.VMEM)] * 2,
        out_specs=pl.BlockSpec(memory_space=pltpu.VMEM),
        compiler_params=pltpu.CompilerParams(vmem_limit_bytes=24 << 20),
        cost_estimate=cost(2 * rows * length * count * width, 4 * rows * width),
        name="dispatch",
    )(routes.reshape(1, count), planes)


BLOCK_ROWS = 256
CHUNK = 32
TRAIN_VMEM = 38 << 20


def train_kernel(
    recv_ref, one_far, two_far,
    ch1_ref, ch2_ref,
    hn_ref, eb_ref, u2_ref, xb, a_ref, gram, z_ref, h_ref, sp_ref, r_ref, y_ref, ef_ref, g_ref, sum_ref, w2_ref, one_ref, two_ref, sems,
):
    one_copy = pltpu.make_async_copy(one_far, one_ref, sems.at[0])
    two_copy = pltpu.make_async_copy(two_far, two_ref, sems.at[1])
    one_copy.start()
    two_copy.start()
    width = recv_ref.shape[1]
    total = recv_ref.shape[0]
    slots = total // 4
    rows = 3 * slots
    c = width**-0.5
    blocks = rows // BLOCK_ROWS
    i = lax.broadcasted_iota(jnp.int32, (128, 128), 0)
    j = lax.broadcasted_iota(jnp.int32, (128, 128), 1)
    source = ((i % 32) // 2) * 8 + (i // 32) * 2 + i % 2
    perm = jnp.where(j == source, 1.0, 0.0).astype(bf16)
    empties = jnp.zeros((1, 128), f32)
    for b in range(total // 128):
        v = recv_ref[b * 128 : (b + 1) * 128, :].astype(f32)
        gone = v > 7.0
        empties = empties + jnp.sum(jnp.where(gone[:, :128], 1.0, 0.0), axis=0, keepdims=True)
        v = jnp.where(gone, 0.0, v).astype(bf16)
        p = jnp.dot(perm, v, preferred_element_type=f32).astype(bf16)
        for t in range(4):
            xb[t * slots + b * 32 : t * slots + (b + 1) * 32, :] = p[t * 32 : (t + 1) * 32, :]
    valid = slots - jnp.max(empties, axis=1, keepdims=True) * 0.25
    inv = 1.0 / (3.0 * valid)
    k = inner_rate * c * inv

    def chunks(b, size=CHUNK):
        for q in range(BLOCK_ROWS // size):
            at = b * BLOCK_ROWS + q * size
            yield slice(at, at + size)

    for b in range(blocks):
        for s in chunks(b):
            x = xb[s, :].astype(f32)
            r = lax.rsqrt(jnp.sum(x * x, axis=1, keepdims=True) * (1.0 / width) + 1e-6)
            a_ref[s, :] = (x * r).astype(bf16)

    def block(b):
        return slice(b * BLOCK_ROWS, (b + 1) * BLOCK_ROWS)

    one_copy.wait()
    for b in range(blocks):
        z_ref[block(b), :] = jnp.dot(a_ref[block(b), :], one_ref[...], preferred_element_type=f32)
    for b in range(blocks):
        gram[block(b), :] = lax.dot_general(
            a_ref[block(b), :], a_ref[...], (((1,), (1,)), ((), ())), preferred_element_type=f32
        ).astype(bf16)

    def hidden(s, step):
        if step == 0:
            z = z_ref[s, :] * c
        else:
            z = z_ref[s, :] - y_ref[s, :]
        if step < STEPS - 1:
            z_ref[s, :] = z
        sg = 0.5 * jnp.tanh(0.5 * z) + 0.5
        si = z * sg
        h = xb[s, :].astype(f32) + si
        sp_ref[s, :] = (sg + si * (1.0 - sg)) * c
        r = lax.rsqrt(jnp.sum(h * h, axis=1, keepdims=True) * (1.0 / width) + 1e-6)
        h_ref[s, :] = h
        r_ref[s, :] = jnp.broadcast_to(r, (h.shape[0], 128))
        hn_ref[s, :] = (h * r).astype(bf16)

    def error(s):
        t = xb[s.start + slots : s.stop + slots, :].astype(f32)
        ef = (h_ref[s, :] + c * y_ref[s, :] - t) * k
        ef_ref[s, :] = ef
        eb_ref[s, :] = ef.astype(bf16)

    def back(s, step):
        q, h, r = y_ref[s, :], h_ref[s, :], r_ref[s, :1]
        qh = jnp.sum(q * h, axis=1, keepdims=True)
        m = (c / width) * r * r * r * qh
        g = sp_ref[s, :] * (ef_ref[s, :] + (c * r) * q - m * h)
        if step == 0:
            sum_ref[s, :] = g
        elif step < STEPS - 1:
            sum_ref[s, :] = sum_ref[s, :] + g
        else:
            g = sum_ref[s, :] + g
        g_ref[s, :] = g.astype(bf16)

    two_copy.wait()
    w2 = two_ref
    columns = [slice(q * 128, (q + 1) * 128) for q in range(width // 128)]
    for step in range(STEPS):
        last = step == STEPS - 1
        for b in range(blocks):
            for s in chunks(b):
                hidden(s, step)
            y_ref[block(b), :] = jnp.dot(hn_ref[block(b), :], w2[...], preferred_element_type=f32)
        for b in range(blocks):
            for s in chunks(b):
                error(s)
            y_ref[block(b), :] = lax.dot_general(
                eb_ref[block(b), :], w2[...], (((1,), (1,)), ((), ())), preferred_element_type=f32
            )
        for s in columns:
            u2 = first_turned(hn_ref[:, s], eb_ref[...])
            if step > 0:
                u2 = u2_ref[s, :] + u2
            if last:
                ch2_ref[s, :] = u2.astype(bf16)
            else:
                u2_ref[s, :] = u2
        for b in range(blocks):
            for s in chunks(b):
                back(s, step)
        if not last:
            for s in columns:
                w2_ref[s, :] = (two_ref[s, :].astype(f32) - u2_ref[s, :]).astype(bf16)
            w2 = w2_ref
            for b in range(blocks):
                y_ref[block(b), :] = jnp.dot(gram[block(b), :], g_ref[...], preferred_element_type=f32)
    piece = width // 8
    for s in columns:
        d1 = (first_turned(a_ref[:, s], g_ref[...]) * (1.0 / c)).astype(bf16)
        at = s.start
        while at < s.stop:
            n = at // piece
            end = min(s.stop, (n + 1) * piece)
            to = (n % 4 * 2 + n // 4) * piece + at % piece
            ch1_ref[to : to + end - at, :] = d1[at - s.start : end - s.start, :]
            at = end


def first_turned(a, b):
    return lax.dot_general(a, b, (((0,), (0,)), ((), ())), preferred_element_type=f32)


def train(recv, one, two):
    total, width = recv.shape
    rows = total // 4 * 3
    wide, thin, square = ((rows, width), f32), ((rows, width), bf16), (width, width)
    kept = [
        thin, thin, (square, f32),
        ((total, width), bf16), thin, ((rows, rows), bf16), wide, wide, wide,
        ((rows, 128), f32), wide, wide, thin, wide, (square, bf16), (square, bf16), (square, bf16),
    ]
    spec = pl.BlockSpec(memory_space=pltpu.VMEM)
    return pl.pallas_call(
        train_kernel,
        out_shape=[jax.ShapeDtypeStruct(square, bf16)] * 2,
        in_specs=[spec] + [pl.BlockSpec(memory_space=pltpu.HBM)] * 2,
        out_specs=[spec] * 2,
        scratch_shapes=[pltpu.VMEM(*m) for m in kept] + [pltpu.SemaphoreType.DMA((2,))],
        compiler_params=pltpu.CompilerParams(vmem_limit_bytes=TRAIN_VMEM),
        cost_estimate=cost(14 * 2 * rows * width * width, 30 * rows * width),
        name="train",
    )(recv, one, two)


def a2a(array, axis):
    return lax.all_to_all(array, axis, 0, 0, tiled=True)


def swap(array, bit):
    n = lax.axis_size("col")
    return lax.ppermute(array, "col", [(i, i ^ bit) for i in range(n)])


Z_BIT, Y_BITS, CORE_BIT = 8, (2, 4, 6), 1


def assemble_kernel(places_ref, near_ref, far_ref, out_ref):
    n = near_ref.shape[0]
    for k in range(n):
        out_ref[places_ref[k]] = near_ref[k]
        out_ref[places_ref[n + k]] = far_ref[k]


def gather_near(own, other):
    pair = jnp.stack([own, other])
    return jnp.concatenate([pair, *(swap(pair, bit) for bit in Y_BITS)])


def gather_far(near):
    me = lax.axis_index("col")
    far = swap(near, CORE_BIT)
    order = jnp.array([y | z for y in (0, *Y_BITS) for z in (0, Z_BIT)], jnp.int32)
    places = jnp.concatenate([me ^ order, me ^ order ^ CORE_BIT])
    n = 2 * near.shape[0]
    return pl.pallas_call(
        assemble_kernel,
        out_shape=jax.ShapeDtypeStruct((n, *near.shape[1:]), near.dtype),
        in_specs=[pl.BlockSpec(memory_space=pltpu.SMEM)] + [pl.BlockSpec(memory_space=pltpu.VMEM)] * 2,
        out_specs=pl.BlockSpec(memory_space=pltpu.VMEM),
        compiler_params=pltpu.CompilerParams(vmem_limit_bytes=8 << 20),
        cost_estimate=cost(0, 2 * n * near.shape[1] * near.shape[2] * 2),
        name="assemble",
    )(places, near, far)


def pick(array, at, axis):
    return lax.dynamic_index_in_dim(array, at, axis, keepdims=False)


def reduce_one(change):
    me = lax.axis_index("col").astype(jnp.uint32)
    z, y, core = me >> 3, (me >> 1) & 3, me & 1
    width = change.shape[1]
    tiles = change.reshape(4, 2, 2, -1, width)
    got = swap(pick(tiles, core ^ 1, 2), CORE_BIT)
    part = (pick(tiles, core, 2).astype(f32) + got.astype(f32)).astype(bf16)
    got = [swap(pick(part, y ^ jnp.uint32(bit // 2), 0), bit) for bit in Y_BITS]
    part = pick(part, y, 0).astype(f32)
    for g in got:
        part = part + g.astype(f32)
    part = part.astype(bf16)
    got = swap(pick(part, z ^ 1, 0), Z_BIT)
    return pick(part, z, 0), got


def shards(docs, routes, level_one, level_two, moment_one, moment_two):
    n_row = lax.axis_size("row")
    n_col = lax.axis_size("col")
    count, length, width = docs.shape
    own_one = level_one[0].astype(bf16)
    other_one = swap(own_one, Z_BIT)
    own_two = level_two.astype(bf16)
    sent_two = jnp.broadcast_to(own_two, (n_row, *own_two.shape[1:]))
    other_one, sent_two = lax.optimization_barrier((other_one, sent_two))
    whole_two = a2a(sent_two, "row").reshape(width, width)
    outgoing = dispatch(routes, docs)
    near = gather_near(own_one, other_one)
    near, outgoing = lax.optimization_barrier((near, outgoing))
    whole_one = gather_far(near).reshape(width, width)
    recv = a2a(outgoing.reshape(n_row * n_col, length * CAPACITY, width), ("row", "col"))
    change_one, change_two = train(recv.reshape(-1, width), whole_one, whole_two)
    part, got_one = reduce_one(change_one)
    got_two = a2a(change_two.reshape(n_row, -1, width), "row")
    delta_two = (jnp.sum(got_two.astype(f32), axis=0) / n_row)[None]
    next_moment_two = momentum_decay * moment_two + delta_two
    new_two = level_two - outer_rate * (delta_two + momentum_decay * next_moment_two)
    got_one, new_two, next_moment_two = lax.optimization_barrier((got_one, new_two, next_moment_two))
    delta_one = ((part.astype(f32) + got_one.astype(f32)) / n_col)[None]
    next_moment_one = momentum_decay * moment_one + delta_one
    new_one = level_one - outer_rate * (delta_one + momentum_decay * next_moment_one)
    return (new_one, new_two, next_moment_one, next_moment_two)


def solution(mesh):
    placed = (
        P(("row", "col"), None, None),
        P(("row", "col"), None),
        P("row", "col", None),
        P("col", "row", None),
        P("row", "col", None),
        P("col", "row", None),
    )
    return jax.shard_map(
        shards,
        mesh=mesh,
        in_specs=placed,
        out_specs=(
            P("row", "col", None),
            P("col", "row", None),
            P("row", "col", None),
            P("col", "row", None),
        ),
        check_vma=False,
    )
```

```python
import functools

import jax
import jax.numpy as jnp
from jax import lax
from jax.experimental import pallas as pl
from jax.experimental.pallas import tpu as pltpu
from jax.sharding import PartitionSpec as P

STEPS = 3
inner_rate = 64.0
outer_rate = 0.7
momentum_decay = 0.9
EMPTY = 16.0
CAPACITY = 2

f32, bf16 = jnp.float32, jnp.bfloat16


def dispatch_kernel(length, routes_ref, docs_ref, out_ref):
    count = routes_ref.shape[1]
    rows = out_ref.shape[0]
    per = length * CAPACITY
    route = jnp.broadcast_to(routes_ref[...].astype(f32), (count, count))
    turned = route.T
    i = lax.broadcasted_iota(jnp.int32, (count, count), 0)
    j = lax.broadcasted_iota(jnp.int32, (count, count), 1)
    earlier = jnp.where((route == turned) & (i < j), 1.0, 0.0)
    rank = jnp.sum(earlier, axis=0, keepdims=True)
    key = (routes_ref[...].astype(f32) * per + rank).astype(jnp.int32)
    keys = jnp.concatenate([key + CAPACITY * t for t in range(length)], axis=1)
    step = 256
    for b in range(rows // step):
        at = lax.broadcasted_iota(jnp.int32, (step, length * count), 0) + b * step
        hot = jnp.where(at == keys, 1.0, 0.0)
        filled = jnp.sum(hot, axis=1, keepdims=True)
        moved = jnp.dot(hot.astype(bf16), docs_ref[...], preferred_element_type=f32)
        out_ref[b * step : (b + 1) * step, :] = (moved + EMPTY * (1.0 - filled)).astype(bf16)


def cost(flops, moved):
    return pl.CostEstimate(flops=flops, transcendentals=0, bytes_accessed=moved)


def dispatch(routes, docs):
    count, length, width = docs.shape
    paths = count
    planes = jnp.transpose(docs, (1, 0, 2)).reshape(length * count, width)
    rows = 128 * length * CAPACITY
    return pl.pallas_call(
        functools.partial(dispatch_kernel, length),
        out_shape=jax.ShapeDtypeStruct((rows, width), bf16),
        in_specs=[pl.BlockSpec(memory_space=pltpu.VMEM)] * 2,
        out_specs=pl.BlockSpec(memory_space=pltpu.VMEM),
        compiler_params=pltpu.CompilerParams(vmem_limit_bytes=24 << 20),
        cost_estimate=cost(2 * rows * length * count * width, 4 * rows * width),
        name="dispatch",
    )(routes.reshape(1, count), planes)


BLOCK_ROWS = 256
CHUNK = 32
TRAIN_VMEM = 53 << 20


def train_kernel(
    recv_ref, one_far, two_far,
    ch1_out, ch2_out,
    ch1_ref, ch2_ref, hn_ref, eb_ref, u2_ref, xb, a_ref, gram, z_ref, h_ref, sp_ref, r_ref, y_ref, ef_ref, g_ref, sum_ref, w2_ref, one_ref, two_ref, sems,
):
    one_copy = pltpu.make_async_copy(one_far, one_ref, sems.at[0])
    two_copy = pltpu.make_async_copy(two_far, two_ref, sems.at[1])
    one_copy.start()
    two_copy.start()
    width = recv_ref.shape[1]
    total = recv_ref.shape[0]
    slots = total // 4
    rows = 3 * slots
    c = width**-0.5
    blocks = rows // BLOCK_ROWS
    i = lax.broadcasted_iota(jnp.int32, (128, 128), 0)
    j = lax.broadcasted_iota(jnp.int32, (128, 128), 1)
    source = ((i % 32) // 2) * 8 + (i // 32) * 2 + i % 2
    perm = jnp.where(j == source, 1.0, 0.0).astype(bf16)
    empties = jnp.zeros((1, 128), f32)
    for b in range(total // 128):
        v = recv_ref[b * 128 : (b + 1) * 128, :].astype(f32)
        gone = v > 7.0
        empties = empties + jnp.sum(jnp.where(gone[:, :128], 1.0, 0.0), axis=0, keepdims=True)
        v = jnp.where(gone, 0.0, v).astype(bf16)
        p = jnp.dot(perm, v, preferred_element_type=f32).astype(bf16)
        for t in range(4):
            xb[t * slots + b * 32 : t * slots + (b + 1) * 32, :] = p[t * 32 : (t + 1) * 32, :]
    valid = slots - jnp.max(empties, axis=1, keepdims=True) * 0.25
    inv = 1.0 / (3.0 * valid)
    k = inner_rate * c * inv

    def chunks(b, size=CHUNK):
        for q in range(BLOCK_ROWS // size):
            at = b * BLOCK_ROWS + q * size
            yield slice(at, at + size)

    for b in range(blocks):
        for s in chunks(b):
            x = xb[s, :].astype(f32)
            r = lax.rsqrt(jnp.sum(x * x, axis=1, keepdims=True) * (1.0 / width) + 1e-6)
            a_ref[s, :] = (x * r).astype(bf16)

    def block(b):
        return slice(b * BLOCK_ROWS, (b + 1) * BLOCK_ROWS)

    one_copy.wait()
    for b in range(blocks):
        z_ref[block(b), :] = jnp.dot(a_ref[block(b), :], one_ref[...], preferred_element_type=f32)
    for b in range(blocks):
        gram[block(b), :] = lax.dot_general(
            a_ref[block(b), :], a_ref[...], (((1,), (1,)), ((), ())), preferred_element_type=f32
        ).astype(bf16)

    def hidden(s, step):
        if step == 0:
            z = z_ref[s, :] * c
        else:
            z = z_ref[s, :] - y_ref[s, :]
        if step < STEPS - 1:
            z_ref[s, :] = z
        sg = 0.5 * jnp.tanh(0.5 * z) + 0.5
        si = z * sg
        h = xb[s, :].astype(f32) + si
        sp_ref[s, :] = (sg + si * (1.0 - sg)) * c
        r = lax.rsqrt(jnp.sum(h * h, axis=1, keepdims=True) * (1.0 / width) + 1e-6)
        h_ref[s, :] = h
        r_ref[s, :] = jnp.broadcast_to(r, (h.shape[0], 128))
        hn_ref[s, :] = (h * r).astype(bf16)

    def error(s):
        t = xb[s.start + slots : s.stop + slots, :].astype(f32)
        ef = (h_ref[s, :] + c * y_ref[s, :] - t) * k
        ef_ref[s, :] = ef
        eb_ref[s, :] = ef.astype(bf16)

    def back(s, step):
        q, h, r = y_ref[s, :], h_ref[s, :], r_ref[s, :1]
        qh = jnp.sum(q * h, axis=1, keepdims=True)
        m = (c / width) * r * r * r * qh
        g = sp_ref[s, :] * (ef_ref[s, :] + (c * r) * q - m * h)
        if step == 0:
            sum_ref[s, :] = g
        elif step < STEPS - 1:
            sum_ref[s, :] = sum_ref[s, :] + g
        else:
            g = sum_ref[s, :] + g
        g_ref[s, :] = g.astype(bf16)

    two_copy.wait()
    w2 = two_ref
    sent = []

    def send(kept, out, start, size):
        copy = pltpu.make_async_copy(
            kept.at[pl.ds(start, size), :], out.at[pl.ds(start, size), :], sems.at[2 + len(sent)]
        )
        copy.start()
        sent.append(copy)

    columns = [slice(q * 128, (q + 1) * 128) for q in range(width // 128)]
    for step in range(STEPS):
        last = step == STEPS - 1
        for b in range(blocks):
            for s in chunks(b):
                hidden(s, step)
            y_ref[block(b), :] = jnp.dot(hn_ref[block(b), :], w2[...], preferred_element_type=f32)
        for b in range(blocks):
            for s in chunks(b):
                error(s)
            y_ref[block(b), :] = lax.dot_general(
                eb_ref[block(b), :], w2[...], (((1,), (1,)), ((), ())), preferred_element_type=f32
            )
        for s in columns:
            u2 = first_turned(hn_ref[:, s], eb_ref[...])
            if step > 0:
                u2 = u2_ref[s, :] + u2
            if last:
                ch2_ref[s, :] = u2.astype(bf16)
                send(ch2_ref, ch2_out, s.start, 128)
            else:
                u2_ref[s, :] = u2
        for b in range(blocks):
            for s in chunks(b):
                back(s, step)
        if not last:
            for s in columns:
                w2_ref[s, :] = (two_ref[s, :].astype(f32) - u2_ref[s, :]).astype(bf16)
            w2 = w2_ref
            for b in range(blocks):
                y_ref[block(b), :] = jnp.dot(gram[block(b), :], g_ref[...], preferred_element_type=f32)
    piece = width // 8
    for s in columns:
        d1 = (first_turned(a_ref[:, s], g_ref[...]) * (1.0 / c)).astype(bf16)
        at = s.start
        while at < s.stop:
            n = at // piece
            end = min(s.stop, (n + 1) * piece)
            to = (n % 4 * 2 + n // 4) * piece + at % piece
            ch1_ref[to : to + end - at, :] = d1[at - s.start : end - s.start, :]
            if end % piece == 0:
                send(ch1_ref, ch1_out, to + end - at - piece, piece)
            at = end
    for copy in sent:
        copy.wait()


def first_turned(a, b):
    return lax.dot_general(a, b, (((0,), (0,)), ((), ())), preferred_element_type=f32)


def train(recv, one, two):
    total, width = recv.shape
    rows = total // 4 * 3
    wide, thin, square = ((rows, width), f32), ((rows, width), bf16), (width, width)
    kept = [
        (square, bf16), (square, bf16), thin, thin, (square, f32),
        ((total, width), bf16), thin, ((rows, rows), bf16), wide, wide, wide,
        ((rows, 128), f32), wide, wide, thin, wide, (square, bf16), (square, bf16), (square, bf16),
    ]
    spec = pl.BlockSpec(memory_space=pltpu.VMEM)
    return pl.pallas_call(
        train_kernel,
        out_shape=[jax.ShapeDtypeStruct(square, bf16)] * 2,
        in_specs=[spec] + [pl.BlockSpec(memory_space=pltpu.HBM)] * 2,
        out_specs=[pl.BlockSpec(memory_space=pltpu.HBM)] * 2,
        scratch_shapes=[pltpu.VMEM(*m) for m in kept] + [pltpu.SemaphoreType.DMA((2 + 8 + width // 128,))],
        compiler_params=pltpu.CompilerParams(vmem_limit_bytes=TRAIN_VMEM),
        cost_estimate=cost(14 * 2 * rows * width * width, 30 * rows * width),
        name="train",
    )(recv, one, two)


def a2a(array, axis):
    return lax.all_to_all(array, axis, 0, 0, tiled=True)


def swap(array, bit):
    n = lax.axis_size("col")
    return lax.ppermute(array, "col", [(i, i ^ bit) for i in range(n)])


Z_BIT, Y_BITS, CORE_BIT = 8, (2, 4, 6), 1


def assemble_kernel(places_ref, near_ref, far_ref, out_ref):
    n = near_ref.shape[0]
    for k in range(n):
        out_ref[places_ref[k]] = near_ref[k]
        out_ref[places_ref[n + k]] = far_ref[k]


def gather_near(own, other):
    pair = jnp.stack([own, other])
    return jnp.concatenate([pair, *(swap(pair, bit) for bit in Y_BITS)])


def gather_far(near):
    me = lax.axis_index("col")
    far = swap(near, CORE_BIT)
    order = jnp.array([y | z for y in (0, *Y_BITS) for z in (0, Z_BIT)], jnp.int32)
    places = jnp.concatenate([me ^ order, me ^ order ^ CORE_BIT])
    n = 2 * near.shape[0]
    return pl.pallas_call(
        assemble_kernel,
        out_shape=jax.ShapeDtypeStruct((n, *near.shape[1:]), near.dtype),
        in_specs=[pl.BlockSpec(memory_space=pltpu.SMEM)] + [pl.BlockSpec(memory_space=pltpu.VMEM)] * 2,
        out_specs=pl.BlockSpec(memory_space=pltpu.VMEM),
        compiler_params=pltpu.CompilerParams(vmem_limit_bytes=8 << 20),
        cost_estimate=cost(0, 2 * n * near.shape[1] * near.shape[2] * 2),
        name="assemble",
    )(places, near, far)


def pick(array, at, axis):
    return lax.dynamic_index_in_dim(array, at, axis, keepdims=False)


def reduce_one(change):
    me = lax.axis_index("col").astype(jnp.uint32)
    z, y, core = me >> 3, (me >> 1) & 3, me & 1
    width = change.shape[1]
    tiles = change.reshape(4, 2, 2, -1, width)
    got = swap(pick(tiles, core ^ 1, 2), CORE_BIT)
    part = (pick(tiles, core, 2).astype(f32) + got.astype(f32)).astype(bf16)
    got = [swap(pick(part, y ^ jnp.uint32(bit // 2), 0), bit) for bit in Y_BITS]
    part = pick(part, y, 0).astype(f32)
    for g in got:
        part = part + g.astype(f32)
    part = part.astype(bf16)
    got = swap(pick(part, z ^ 1, 0), Z_BIT)
    return pick(part, z, 0), got


def shards(docs, routes, level_one, level_two, moment_one, moment_two):
    n_row = lax.axis_size("row")
    n_col = lax.axis_size("col")
    count, length, width = docs.shape
    own_one = level_one[0].astype(bf16)
    other_one = swap(own_one, Z_BIT)
    own_two = level_two.astype(bf16)
    sent_two = jnp.broadcast_to(own_two, (n_row, *own_two.shape[1:]))
    other_one, sent_two = lax.optimization_barrier((other_one, sent_two))
    whole_two = a2a(sent_two, "row").reshape(width, width)
    outgoing = dispatch(routes, docs)
    near = gather_near(own_one, other_one)
    near, outgoing = lax.optimization_barrier((near, outgoing))
    whole_one = gather_far(near).reshape(width, width)
    recv = a2a(outgoing.reshape(n_row * n_col, length * CAPACITY, width), ("row", "col"))
    change_one, change_two = train(recv.reshape(-1, width), whole_one, whole_two)
    part, got_one = reduce_one(change_one)
    got_two = a2a(change_two.reshape(n_row, -1, width), "row")
    delta_two = (jnp.sum(got_two.astype(f32), axis=0) / n_row)[None]
    next_moment_two = momentum_decay * moment_two + delta_two
    new_two = level_two - outer_rate * (delta_two + momentum_decay * next_moment_two)
    got_one, new_two, next_moment_two = lax.optimization_barrier((got_one, new_two, next_moment_two))
    delta_one = ((part.astype(f32) + got_one.astype(f32)) / n_col)[None]
    next_moment_one = momentum_decay * moment_one + delta_one
    new_one = level_one - outer_rate * (delta_one + momentum_decay * next_moment_one)
    return (new_one, new_two, next_moment_one, next_moment_two)


def solution(mesh):
    placed = (
        P(("row", "col"), None, None),
        P(("row", "col"), None),
        P("row", "col", None),
        P("col", "row", None),
        P("row", "col", None),
        P("col", "row", None),
    )
    return jax.shard_map(
        shards,
        mesh=mesh,
        in_specs=placed,
        out_specs=(
            P("row", "col", None),
            P("col", "row", None),
            P("row", "col", None),
            P("col", "row", None),
        ),
        check_vma=False,
    )
```
